128 devices in a mesh: seq: 16 (over z, x), exp: 8 (over y, core).
Axes of the slice: x: 4, y: 4, z: 4, core: 2. Of those that a mesh axis runs over, the one named last changes fastest.
Arguments:
- residual: bfloat16 [8192, 8192], P('seq', 'exp'), may hold values from -16 to 16
- queries: bfloat16 [8192, 4096], P('seq', 'exp'), may hold values from -6 to 6
- keys: bfloat16 [8192, 4096], P('seq', 'exp'), may hold values from -10 to 10
- values: bfloat16 [8192, 4096], P('seq', 'exp'), may hold values from -6 to 6
- documents: int32 [8192], replicated, may hold values from 0 to 1, as said below
- out_proj: bfloat16 [4096, 8192], P(None, 'exp'), may hold values from -0.09375 to 0.09375
- modality: int32 [8192], P('seq'), may hold values from 0 to 1, as said below
- norm_gain: float32 [2, 8192], P(None, 'exp'), may hold values from 0.25 to 1.75
- picks: int32 [8, 128], replicated, may hold values from 0 to 8191, as said below
- router: bfloat16 [8192, 8], P(None, 'exp'), may hold values from -0.0625 to 0.0625
- w_gate: bfloat16 [8, 8192, 4096], P('exp', None, 'seq'), may hold values from -0.0625 to 0.0625
- w_up: bfloat16 [8, 8192, 4096], P('exp', None, 'seq'), may hold values from -0.0625 to 0.0625
- w_down: bfloat16 [8, 4096, 8192], P('exp', 'seq'), may hold values from -0.09375 to 0.09375
Outputs:
- layer_out: bfloat16 [8192, 8192], P('seq', 'exp')
The draws below stay inside these ranges and needn't reach their ends.
Inputs may be any that keep to these rules, and one draw needn't show every extreme that they name: `modality`: 0 marks a text token, 1 an image token. `documents`: 0 for the first document, 1 for the second; the second begins between position 2048 and 6144. `picks`: row e lists 128 different positions in ascending order; all carry modality 0 for e < 4 and modality 1 otherwise. Within each aligned block of 512 positions (the tokens of one index of seq) a row lists at most 16 positions, and every row lists exactly 16 in some block.
All inputs are finite; a program needn't handle non-finite values.
Results may differ from the reference program's by a relative error of at most 0.0035.
Values may be sent and summed in bfloat16 or wider, within the bound.
No kernel may reach another device: no remote copies, remote signals or barrier semaphores. Data moves between devices by JAX's collectives and lax.ppermute only.
A program may use at most 128 MiB of HBM per device.

```python
import math
import jax
import jax.numpy as jnp
from jax import lax

D = 8192
HEADS = 32
HD = 128
FF = 4096
TOK_DEV = 512
TOKENS = 8192
EXPERTS = 8
CB = 16
CAP = 128
N_SEQ = 16


def layout_draw(base_key):
    own_key = jax.random.fold_in(base_key, 11)
    span_key, force_key, pick_key = jax.random.split(own_key, 3)
    spans = 8
    span_len = TOK_DEV // spans
    span_bits = jax.random.randint(span_key, (N_SEQ, spans), 0, 2)
    one_key, two_key = jax.random.split(force_key)
    fixed_one = jax.random.randint(one_key, (N_SEQ,), 0, spans)
    offset = jax.random.randint(two_key, (N_SEQ,), 1, spans)
    second = (fixed_one + offset) % spans
    span_pos = jnp.arange(spans)
    span_bits = jnp.where(span_pos[None, :] == fixed_one[:, None], 0, span_bits)
    span_bits = jnp.where(span_pos[None, :] == second[:, None], 1, span_bits)
    modal_tags = jnp.repeat(span_bits, span_len, axis=1).astype(jnp.int32)
    flat_index = jnp.arange(TOKENS, dtype=jnp.int32)
    half_cap = CB // 2
    chosen_lists = []
    for expert in range(EXPERTS):
        modal_kind = 0 if expert < EXPERTS // 2 else 1
        order_key, shift_key, rank_key = jax.random.split(jax.random.fold_in(pick_key, expert), 3)
        shard_order = jax.random.permutation(order_key, N_SEQ)
        shift_size = jax.random.randint(shift_key, (N_SEQ // 2,), 0, half_cap + 1)
        shift_size = shift_size.at[0].set(half_cap)
        quota_rows = jnp.zeros((N_SEQ,), jnp.int32)
        quota_rows = quota_rows.at[shard_order[0::2]].set(half_cap + shift_size)
        quota_rows = quota_rows.at[shard_order[1::2]].set(half_cap - shift_size)
        shuffled = jax.vmap(lambda sub_key: jax.random.permutation(sub_key, TOK_DEV))(jax.random.split(rank_key, N_SEQ))
        sort_keys = jnp.where(modal_tags == modal_kind, shuffled, TOK_DEV + shuffled)
        rank_in = jnp.argsort(jnp.argsort(sort_keys, axis=1), axis=1)
        chosen = (rank_in < quota_rows[:, None]).reshape(TOKENS)
        listed = jnp.argsort(jnp.where(chosen, flat_index, TOKENS + flat_index))[:CAP]
        chosen_lists.append(listed.astype(jnp.int32))
    return (modal_tags.reshape(TOKENS), jnp.stack(chosen_lists))


def draw_modality(key, part):
    return layout_draw(key)[0]


def draw_picks(key, part):
    return layout_draw(key)[1]


def draw_documents(key, part):
    boundary = jax.random.randint(jax.random.fold_in(key, 5), (), TOKENS // 4, 3 * TOKENS // 4 + 1)
    return (jnp.arange(TOKENS) >= boundary).astype(jnp.int32)


def draw_queries(key, part):
    base_key = jax.random.fold_in(key, 31)
    base_draw = jnp.clip(jax.random.normal(base_key, (TOKENS, HEADS * HD), jnp.float32), -6.0, 6.0)
    return base_draw.astype(jnp.bfloat16)


def draw_keys(key, part):
    base_key = jax.random.fold_in(key, 41)
    base_draw = jnp.clip(2.5 * jax.random.normal(base_key, (TOKENS, HEADS * HD), jnp.float32), -10.0, 10.0)
    return base_draw.astype(jnp.bfloat16)


def draw_residual(key, part):
    base_key = jax.random.fold_in(jax.random.fold_in(key, 51), 0)
    rising = 0.6 + 1.2 * jnp.arange(D, dtype=jnp.float32) / D
    base_draw = jnp.clip(jax.random.normal(base_key, (TOKENS, D), jnp.float32), -4.0, 4.0)
    result = base_draw * rising[None, :]
    return jnp.clip(result, -16.0, 16.0).astype(jnp.bfloat16)


def shard_levels(key, extent, shards, smallest, top_value):
    def one(position, blocks):
        heights = jax.random.uniform(jax.random.fold_in(jax.random.fold_in(key, 6), position), (blocks,), jnp.float32, smallest / len(shards), top_value / len(shards))
        return jnp.repeat(jnp.exp(heights), extent[position] // blocks).reshape((-1,) + (1,) * (len(extent) - position - 1))

    gain = one(*shards[0])
    for cut in shards[1:]:
        gain = gain * one(*cut)
    return gain


def bell_draw(key, extent, deviation, limit, cuts=(), kind=jnp.bfloat16):
    level = shard_levels(key, extent, cuts, -0.22, 0.18) if cuts else 1.0
    entries = jax.random.normal(key, extent, jnp.float32) * deviation * level
    return jnp.minimum(jnp.maximum(entries, -limit), limit).astype(kind)


def setup_inputs(seed: int = 0) -> dict:
    arg_keys = jax.random.split(jax.random.key(seed), 14)
    return {
        "residual": draw_residual(jax.random.fold_in(arg_keys[13], 71), 0),
        "queries": draw_queries(jax.random.fold_in(arg_keys[13], 71), 0),
        "keys": draw_keys(jax.random.fold_in(arg_keys[13], 71), 0),
        "values": bell_draw(arg_keys[3], (TOKENS, HEADS * HD), 1.0, 6.0, ((0, 16), (1, 8))),
        "documents": draw_documents(jax.random.fold_in(arg_keys[13], 71), 0),
        "out_proj": bell_draw(arg_keys[5], (HEADS * HD, D), (HEADS * HD) ** -0.5, 0.09375, ((1, 8),)),
        "modality": draw_modality(jax.random.fold_in(arg_keys[13], 71), 0),
        "norm_gain": jnp.clip(1.0 + 0.15 * jax.random.normal(arg_keys[7], (2, D), jnp.float32), 0.25, 1.75),
        "picks": draw_picks(jax.random.fold_in(arg_keys[13], 71), 0),
        "router": bell_draw(arg_keys[9], (D, EXPERTS), D ** -0.5, 0.0625, ((1, 8),)),
        "w_gate": bell_draw(arg_keys[10], (EXPERTS, D, FF), D ** -0.5, 0.0625, ((0, 8), (2, 16))),
        "w_up": bell_draw(arg_keys[11], (EXPERTS, D, FF), D ** -0.5, 0.0625, ((0, 8), (2, 16))),
        "w_down": bell_draw(arg_keys[12], (EXPERTS, FF, D), FF ** -0.5, 0.09375, ((0, 8), (1, 16))),
    }


def reference(residual, queries, keys, values, documents, out_proj, modality, norm_gain, picks, router, w_gate, w_up, w_down):
    length = queries.shape[0]
    q_heads = queries.reshape(length, HEADS, HD).transpose(1, 0, 2)
    k_heads = keys.reshape(length, HEADS, HD).transpose(1, 0, 2)
    v_heads = values.reshape(length, HEADS, HD).transpose(1, 0, 2)
    positions = jnp.arange(length, dtype=jnp.int32)
    allowed = (positions[None, :] <= positions[:, None]) & (documents[None, :] == documents[:, None])

    def one_head(item):
        q_one, k_one, v_one = item
        scores = jnp.dot(q_one, k_one.T, preferred_element_type=jnp.float32) / math.sqrt(HD)
        scores = jnp.where(allowed, scores, -jnp.inf)
        row_max = lax.optimization_barrier(jnp.max(scores, axis=1))
        probs = jnp.exp(scores - row_max[:, None])
        denominator = lax.optimization_barrier(jnp.sum(probs, axis=1))
        numerator = jnp.dot(probs.astype(jnp.bfloat16), v_one, preferred_element_type=jnp.float32)
        return (numerator / denominator[:, None]).astype(jnp.bfloat16)
    attended = lax.map(one_head, (q_heads, k_heads, v_heads))
    attended = attended.transpose(1, 0, 2).reshape(length, HEADS * HD)
    hidden_state = (residual.astype(jnp.float32) + jnp.dot(attended, out_proj, preferred_element_type=jnp.float32)).astype(jnp.bfloat16)
    hidden_wide = hidden_state.astype(jnp.float32)
    mean_square = lax.optimization_barrier(jnp.mean(hidden_wide * hidden_wide, axis=1))
    gain_rows = norm_gain[modality]
    normed = (hidden_wide * lax.rsqrt(mean_square + 1e-05)[:, None] * gain_rows).astype(jnp.bfloat16)
    expert_add = jnp.zeros((length, D), jnp.float32)
    for expert in range(EXPERTS):
        chosen = normed[picks[expert]]
        gate_part = jnp.dot(chosen, w_gate[expert], preferred_element_type=jnp.float32)
        up_part = jnp.dot(chosen, w_up[expert], preferred_element_type=jnp.float32)
        inner_act = (jax.nn.silu(gate_part) * up_part).astype(jnp.bfloat16)
        summed = jnp.dot(inner_act, w_down[expert], preferred_element_type=jnp.float32)
        logits = jnp.dot(chosen, router[:, expert:expert + 1], preferred_element_type=jnp.float32)[:, 0]
        weighted = (jax.nn.sigmoid(logits)[:, None] * summed).astype(jnp.bfloat16)
        expert_add = expert_add.at[picks[expert]].add(weighted.astype(jnp.float32))
    return (hidden_wide + expert_add).astype(jnp.bfloat16)
```

```python
import math

import jax
import jax.numpy as jnp
import numpy as np
from jax import lax
from jax.experimental import pallas as pl
from jax.experimental.pallas import tpu as pltpu
from jax.sharding import Mesh
from jax.sharding import PartitionSpec as P

D = 8192
HD = 128
TOK = 512
BLOCKS = 16
ALL = ("z", "x", "y", "c")
SEQ = ("z", "x")
EXP = ("y", "c")
NEG = -1e30
SCALE = math.log2(math.e) / math.sqrt(HD)

IDS = np.arange(128).reshape(4, 4, 4, 2)


def _groups(first):
    rows = []
    for y in range(4):
        for k in range(4):
            along_z, along_x = IDS[:, k, y, :], IDS[k, :, y, :]
            rows.append([int(i) for i in (along_z if first else along_x)[:, 0]])
            rows.append([int(i) for i in (along_x if first else along_z)[:, 1]])
    return rows


def _group16():
    rows = []
    for y in range(4):
        rows.append([int(i) for i in IDS[:, :, y, 0].reshape(-1)])
        rows.append([int(i) for i in IDS[:, :, y, 1].T.reshape(-1)])
    return rows


GROUP_A = _groups(True)
GROUP_B = _groups(False)
GROUP_AB = _group16()


def exchange(array, groups):
    return lax.all_to_all(array, ALL, 0, 0, tiled=True, axis_index_groups=groups)


def spread(array, groups):
    return exchange(jnp.broadcast_to(array[None], (4, *array.shape)), groups)


def attend_kernel(tab, r, o, vt, s, acc, m, l):
    bound = tab[32]
    sub = tab[33]

    def turn(t, carry):
        vt[t] = r[t, 512:1024, :].T
        return carry

    lax.fori_loop(0, BLOCKS, turn, 0)
    col = lax.broadcasted_iota(jnp.int32, (1, 256), 1)
    row = lax.broadcasted_iota(jnp.int32, (TOK, 1), 0)

    def score(t, q):
        return lax.dot_general(
            r[tab[t], 0:512, :], q, (((1,), (1,)), ((), ())), preferred_element_type=jnp.float32
        )

    def pair(pair_index, carry):
        j = 2 * pair_index
        q = jnp.concatenate([r[tab[j], 1024:1152, :], r[tab[j + 1], 1024:1152, :]], axis=0)
        first = j * TOK + sub * 128
        last = first + TOK + 127
        qpos = first + jnp.where(col < 128, col, col + (TOK - 128))
        qlow = jnp.where(qpos >= bound, bound, 0)
        lo = jnp.where(first >= bound, bound // TOK, 0)
        hi = j + 2
        m[...] = jnp.full((1, 256), NEG, jnp.float32)
        l[...] = jnp.zeros((1, 256), jnp.float32)
        acc[...] = jnp.zeros((HD, 256), jnp.float32)
        s[0] = score(lo, q)

        def step(t, inner):
            now = lax.rem(t - lo, 2)

            def go(masked):
                s[1 - now] = score(jnp.minimum(t + 1, hi - 1), q)
                here = s[now]
                if masked:
                    kpos = t * TOK + row
                    here = jnp.where((kpos <= qpos) & (kpos >= qlow), here, NEG)
                old = m[...]
                new = jnp.maximum(old, jnp.max(here, axis=0, keepdims=True))
                p = jnp.exp2(here * SCALE - new * SCALE)
                f = jnp.exp2((old - new) * SCALE)
                m[...] = new
                l[...] = l[...] * f + jnp.sum(p, axis=0, keepdims=True)
                acc[...] = acc[...] * f + jnp.dot(
                    vt[tab[t]], p.astype(jnp.bfloat16), preferred_element_type=jnp.float32
                )

            need = ((t + 1) * TOK - 1 > first) | ((t * TOK < bound) & (last >= bound))
            pl.when(need)(lambda: go(True))
            pl.when(jnp.logical_not(need))(lambda: go(False))
            return inner

        lax.fori_loop(lo, hi, step, 0)
        out = (acc[...] / l[...]).T.astype(jnp.bfloat16)
        o[tab[16 + j]] = out[:128]
        o[tab[17 + j]] = out[128:]
        return carry

    lax.fori_loop(0, BLOCKS // 2, pair, 0)


def attend(tab, received):
    return pl.pallas_call(
        attend_kernel,
        out_shape=jax.ShapeDtypeStruct((BLOCKS, 128, HD), jnp.bfloat16),
        in_specs=[
            pl.BlockSpec(memory_space=pltpu.SMEM),
            pl.BlockSpec(memory_space=pltpu.VMEM),
        ],
        out_specs=pl.BlockSpec(memory_space=pltpu.VMEM),
        scratch_shapes=[
            pltpu.VMEM((BLOCKS, HD, TOK), jnp.bfloat16),
            pltpu.VMEM((2, TOK, 256), jnp.float32),
            pltpu.VMEM((HD, 256), jnp.float32),
            pltpu.VMEM((1, 256), jnp.float32),
            pltpu.VMEM((1, 256), jnp.float32),
        ],
        compiler_params=pltpu.CompilerParams(vmem_limit_bytes=24 << 20),
        cost_estimate=pl.CostEstimate(
            flops=4_000_000_000, bytes_accessed=5_000_000, transcendentals=6_000_000
        ),
        name="attend",
    )(tab, received)


def project_kernel(c, x, w, base, o, acc, *, last):
    k = pl.program_id(0)

    @pl.when(k == 0)
    def _():
        acc[...] = base[...].astype(jnp.float32)

    acc[...] += jnp.dot(x[0], w[...], preferred_element_type=jnp.float32)

    @pl.when(k == 3)
    def _():
        o[...] = acc[...].astype(o.dtype)


def project(c, x, w, base, last):
    def kernel(c_ref, *refs):
        project_kernel(c_ref, *refs, last=last)

    return pl.pallas_call(
        kernel,
        grid_spec=pltpu.PrefetchScalarGridSpec(
            num_scalar_prefetch=1,
            grid=(4,),
            in_specs=[
                pl.BlockSpec((1, TOK, 512), lambda k, c_ref: (k, 0, 0)),
                pl.BlockSpec((512, 1024), lambda k, c_ref: (2 * k + c_ref[0], 0)),
                pl.BlockSpec((TOK, 1024), lambda k, c_ref: (0, 0), pipeline_mode=pl.Buffered(1)),
            ],
            out_specs=pl.BlockSpec((TOK, 1024), lambda k, c_ref: (0, 0)),
            scratch_shapes=[pltpu.VMEM((TOK, 1024), jnp.float32)],
        ),
        out_shape=jax.ShapeDtypeStruct((TOK, 1024), jnp.bfloat16 if last else jnp.float32),
        compiler_params=pltpu.CompilerParams(vmem_limit_bytes=24 << 20),
        cost_estimate=pl.CostEstimate(
            flops=2_200_000_000, bytes_accessed=9_000_000, transcendentals=0
        ),
        name="project",
    )(c, x, w, base)


def shards(
    residual,
    queries,
    keys,
    values,
    documents,
    out_proj,
    modality,
    norm_gain,
    picks,
    router,
    w_gate,
    w_up,
    w_down,
):
    z, x, y, c = (lax.axis_index(name) for name in ALL)
    seq = z * 4 + x
    expert = y * 2 + c
    b = jnp.where(c == 0, x, z)

    gain_sent = jnp.concatenate(
        [jnp.broadcast_to(norm_gain[k][None], (4, 1024)) for k in range(2)], axis=0
    ).reshape(8, 8, 128)
    gain = lax.all_to_all(gain_sent, EXP, 0, 0, tiled=True).reshape(1, D)

    sent = jnp.stack([a.reshape(TOK, 4, HD) for a in (queries, keys, values)], axis=0)
    got = exchange(sent.transpose(2, 0, 1, 3), GROUP_A)
    both = jnp.broadcast_to(got[:, 1:].reshape(1, 4, 1024, HD), (4, 4, 1024, HD))
    part = got[:, 0].reshape(4, 4, 128, HD).transpose(1, 0, 2, 3)
    received = exchange(jnp.concatenate([both, part], axis=2), GROUP_B)
    received = received.reshape(BLOCKS, 1152, HD)

    index = jnp.arange(BLOCKS, dtype=jnp.int32)
    swapped = (index % 4) * 4 + index // 4
    bound = documents.shape[0] - jnp.sum(documents)
    tab = jnp.concatenate(
        [
            jnp.where(c == 0, swapped, index),
            jnp.where(c == 0, index, swapped),
            jnp.stack([bound, b]).astype(jnp.int32),
        ]
    ).astype(jnp.int32)
    attended = exchange(attend(tab, received), GROUP_AB)
    attended = attended.reshape(4, TOK, HD).transpose(1, 0, 2).reshape(TOK, 4 * HD)

    mine = lax.all_to_all(
        jnp.broadcast_to(attended[None], (4, TOK, 512)), "y", 0, 0, tiled=True
    )
    theirs = lax.ppermute(mine, "c", [(0, 1), (1, 0)])
    core = jnp.reshape(c, (1,)).astype(jnp.int32)
    mixed = project(core, mine, out_proj, residual, False)
    hidden = project(1 - core, theirs, out_proj, mixed, True)

    ranked = picks.reshape(8, 8, 16)
    inside = (ranked // TOK) == seq
    local = jnp.sum(jnp.where(inside, ranked - seq * TOK, 0), axis=1).T.reshape(128, 1)
    filled = jnp.any(inside, axis=1).T.reshape(128, 1)
    hot = ((jnp.arange(TOK, dtype=jnp.int32)[None, :] == local) & filled).astype(jnp.bfloat16)
    rows = jnp.dot(hot, hidden, preferred_element_type=jnp.float32).astype(jnp.bfloat16)
    arrived = lax.all_to_all(rows.reshape(128, 8, 128), ALL, 0, 0, tiled=True)
    own = lax.dynamic_index_in_dim(ranked, expert, 0, keepdims=False)
    own = lax.dynamic_index_in_dim(own, seq, 1, keepdims=False)
    source = (own // TOK)[:, None] == jnp.arange(16, dtype=jnp.int32)[None, :]
    source = source.astype(jnp.bfloat16)
    taken = jnp.dot(source, arrived.reshape(16, D), preferred_element_type=jnp.float32)
    inverse = lax.rsqrt(jnp.mean(taken * taken, axis=1, keepdims=True) + 1e-05)
    chosen = (taken * inverse * gain).astype(jnp.bfloat16)
    logits = jnp.dot(chosen, router, preferred_element_type=jnp.float32)
    near = spread(chosen, GROUP_A)
    far = spread(near.reshape(32, D), GROUP_B)
    piece = far.reshape(128, D)
    gate_part = jnp.dot(piece, w_gate[0], preferred_element_type=jnp.float32)
    up_part = jnp.dot(piece, w_up[0], preferred_element_type=jnp.float32)
    inner_act = (jax.nn.silu(gate_part) * up_part).astype(jnp.bfloat16)
    partial = jnp.dot(inner_act, w_down[0], preferred_element_type=jnp.float32)
    partial = exchange(partial.astype(jnp.bfloat16).reshape(4, 32, D), GROUP_B)
    partial = jnp.sum(partial.astype(jnp.float32), axis=0).astype(jnp.bfloat16)
    partial = exchange(partial.reshape(4, 8, D), GROUP_A)
    summed = jnp.sum(partial.astype(jnp.float32), axis=0)
    weighted = (jax.nn.sigmoid(logits) * summed).astype(jnp.bfloat16)
    back = lax.dot_general(
        source, weighted, (((0,), (0,)), ((), ())), preferred_element_type=jnp.float32
    ).astype(jnp.bfloat16)
    returned = lax.all_to_all(back.reshape(128, 8, 128), ALL, 0, 0, tiled=True)
    expert_add = lax.dot_general(
        hot, returned.reshape(128, 1024), (((0,), (0,)), ((), ())), preferred_element_type=jnp.float32
    )
    return (hidden.astype(jnp.float32) + expert_add).astype(jnp.bfloat16)


def solution(mesh):
    finer = Mesh(mesh.devices.reshape(4, 4, 4, 2), ALL)
    in_specs = (
        P(SEQ, EXP),
        P(SEQ, EXP),
        P(SEQ, EXP),
        P(SEQ, EXP),
        P(),
        P(None, EXP),
        P(SEQ),
        P(None, EXP),
        P(),
        P(None, EXP),
        P(EXP, None, SEQ),
        P(EXP, None, SEQ),
        P(EXP, SEQ, None),
    )
    return jax.shard_map(
        shards, mesh=finer, in_specs=in_specs, out_specs=P(SEQ, EXP), check_vma=False
    )
```

```python
import math

import jax
import jax.numpy as jnp
import numpy as np
from jax import lax
from jax.experimental import pallas as pl
from jax.experimental.pallas import tpu as pltpu
from jax.sharding import Mesh
from jax.sharding import PartitionSpec as P

D = 8192
HD = 128
TOK = 512
BLOCKS = 16
ALL = ("z", "x", "y", "c")
SEQ = ("z", "x")
EXP = ("y", "c")
NEG = -1e30
SCALE = math.log2(math.e) / math.sqrt(HD)

IDS = np.arange(128).reshape(4, 4, 4, 2)


def _groups(first):
    rows = []
    for y in range(4):
        for k in range(4):
            along_z, along_x = IDS[:, k, y, :], IDS[k, :, y, :]
            rows.append([int(i) for i in (along_z if first else along_x)[:, 0]])
            rows.append([int(i) for i in (along_x if first else along_z)[:, 1]])
    return rows


def _group16():
    rows = []
    for y in range(4):
        rows.append([int(i) for i in IDS[:, :, y, 0].reshape(-1)])
        rows.append([int(i) for i in IDS[:, :, y, 1].T.reshape(-1)])
    return rows


GROUP_A = _groups(True)
GROUP_B = _groups(False)
GROUP_AB = _group16()


def exchange(array, groups):
    return lax.all_to_all(array, ALL, 0, 0, tiled=True, axis_index_groups=groups)


def spread(array, groups):
    return exchange(jnp.broadcast_to(array[None], (4, *array.shape)), groups)


def pack_heads_kernel(q, k, v, o):
    for i, ref in enumerate((q, k, v)):
        o[0, i] = ref[...]


def pack_heads(queries, keys, values):
    column = pl.BlockSpec((TOK, HD), lambda h: (0, h))
    return pl.pallas_call(
        pack_heads_kernel,
        grid=(4,),
        in_specs=[column] * 3,
        out_specs=pl.BlockSpec((1, 3, TOK, HD), lambda h: (h, 0, 0, 0)),
        out_shape=jax.ShapeDtypeStruct((4, 3, TOK, HD), jnp.bfloat16),
        name="pack_heads",
    )(queries, keys, values)


def pack_parts_kernel(got, q, o):
    for i in range(4):
        o[0, i, 0:TOK] = got[i, 1]
        o[0, i, TOK : 2 * TOK] = got[i, 2]
        o[0, i, 2 * TOK :] = q[i, 0]


def pack_parts(got):
    return pl.pallas_call(
        pack_parts_kernel,
        grid=(4,),
        in_specs=[
            pl.BlockSpec((4, 3, TOK, HD), lambda p: (0, 0, 0, 0)),
            pl.BlockSpec((4, 1, 128, HD), lambda p: (0, 0, p, 0)),
        ],
        out_specs=pl.BlockSpec((1, 4, 1152, HD), lambda p: (p, 0, 0, 0)),
        out_shape=jax.ShapeDtypeStruct((4, 4, 1152, HD), jnp.bfloat16),
        compiler_params=pltpu.CompilerParams(vmem_limit_bytes=16 << 20),
        name="pack_parts",
    )(got, got)


QW = 512
TILE = QW // 128


def attend_kernel(tab, r, o, vt, s0, s1, acc, m, l, qt):
    bound = tab[32]
    sub = tab[33]

    def turn(t, carry):
        vt[t] = r[t, TOK : 2 * TOK, :].T
        return carry

    lax.fori_loop(0, BLOCKS, turn, 0)
    col = lax.broadcasted_iota(jnp.int32, (1, QW), 1)
    row = lax.broadcasted_iota(jnp.int32, (TOK, 1), 0)

    def score(t):
        return jnp.dot(r[tab[t], 0:TOK, :], qt[...], preferred_element_type=jnp.float32)

    def tile(index, carry):
        j = TILE * index
        for i in range(TILE):
            qt[:, i * 128 : (i + 1) * 128] = r[tab[j + i], 2 * TOK :, :].T
        first = j * TOK + sub * 128
        last = first + (TILE - 1) * TOK + 127
        qpos = first + (col // 128) * TOK + col % 128
        qlow = jnp.where(qpos >= bound, bound, 0)
        lo = jnp.where(first >= bound, bound // (2 * TOK), 0)
        hi = (j + TILE) // 2
        m[...] = jnp.full((1, QW), NEG, jnp.float32)
        l[...] = jnp.zeros((1, QW), jnp.float32)
        acc[...] = jnp.zeros((HD, QW), jnp.float32)
        s0[...] = score(2 * lo)

        def soft(s, t, masked):
            here = s[...]
            if masked:
                kpos = t * TOK + row
                here = jnp.where((kpos <= qpos) & (kpos >= qlow), here, NEG)
            old = m[...]
            new = jnp.maximum(old, jnp.max(here, axis=0, keepdims=True))
            p = jnp.exp2(here * SCALE - new * SCALE)
            f = jnp.exp2((old - new) * SCALE)
            m[...] = new
            l[...] = l[...] * f + jnp.sum(p, axis=0, keepdims=True)
            acc[...] = acc[...] * f + jnp.dot(
                vt[tab[t]], p.astype(jnp.bfloat16), preferred_element_type=jnp.float32
            )

        def step(u, inner):
            t = 2 * u

            def go(masked):
                s1[...] = score(t + 1)
                soft(s0, t, masked)
                s0[...] = score(jnp.minimum(t + 2, j + TILE - 1))
                soft(s1, t + 1, masked)

            need = ((t + 2) * TOK - 1 > first) | ((t * TOK < bound) & (last >= bound))
            pl.when(need)(lambda: go(True))
            pl.when(jnp.logical_not(need))(lambda: go(False))
            return inner

        lax.fori_loop(lo, hi, step, 0)
        out = (acc[...] / l[...]).T.astype(jnp.bfloat16)
        for i in range(TILE):
            o[tab[16 + j + i]] = out[i * 128 : (i + 1) * 128]
        return carry

    lax.fori_loop(0, BLOCKS // TILE, tile, 0)


def attend(tab, received):
    return pl.pallas_call(
        attend_kernel,
        out_shape=jax.ShapeDtypeStruct((BLOCKS, 128, HD), jnp.bfloat16),
        in_specs=[
            pl.BlockSpec(memory_space=pltpu.SMEM),
            pl.BlockSpec(memory_space=pltpu.VMEM),
        ],
        out_specs=pl.BlockSpec(memory_space=pltpu.VMEM),
        scratch_shapes=[
            pltpu.VMEM((BLOCKS, HD, TOK), jnp.bfloat16),
            pltpu.VMEM((TOK, QW), jnp.float32),
            pltpu.VMEM((TOK, QW), jnp.float32),
            pltpu.VMEM((HD, QW), jnp.float32),
            pltpu.VMEM((1, QW), jnp.float32),
            pltpu.VMEM((1, QW), jnp.float32),
            pltpu.VMEM((HD, QW), jnp.bfloat16),
        ],
        compiler_params=pltpu.CompilerParams(vmem_limit_bytes=32 << 20),
        cost_estimate=pl.CostEstimate(
            flops=10_000_000_000, bytes_accessed=5_000_000, transcendentals=8_000_000
        ),
        name="attend",
    )(tab, received)


def project_kernel(order, mine, theirs, w, base, o, acc):
    k = pl.program_id(0)

    @pl.when(k == 0)
    def _():
        acc[...] = base[...].astype(jnp.float32)

    @pl.when(k < 4)
    def _():
        acc[...] += jnp.dot(mine[0], w[...], preferred_element_type=jnp.float32)

    @pl.when(k >= 4)
    def _():
        acc[...] += jnp.dot(theirs[0], w[...], preferred_element_type=jnp.float32)

    @pl.when(k == 7)
    def _():
        o[...] = acc[...].astype(jnp.bfloat16)


def project(order, mine, theirs, w, base):
    rows = base.shape[0]
    return pl.pallas_call(
        project_kernel,
        grid_spec=pltpu.PrefetchScalarGridSpec(
            num_scalar_prefetch=1,
            grid=(8,),
            in_specs=[
                pl.BlockSpec((1, rows, 512), lambda k, order: (jnp.minimum(k, 3), 0, 0)),
                pl.BlockSpec((1, rows, 512), lambda k, order: (jnp.maximum(k - 4, 0), 0, 0)),
                pl.BlockSpec((512, 1024), lambda k, order: (order[k], 0)),
                pl.BlockSpec((rows, 1024), lambda k, order: (0, 0)),
            ],
            out_specs=pl.BlockSpec((rows, 1024), lambda k, order: (0, 0)),
            scratch_shapes=[pltpu.VMEM((rows, 1024), jnp.float32)],
        ),
        out_shape=jax.ShapeDtypeStruct((rows, 1024), jnp.bfloat16),
        compiler_params=pltpu.CompilerParams(vmem_limit_bytes=24 << 20),
        cost_estimate=pl.CostEstimate(
            flops=rows * 8_388_608, bytes_accessed=8_388_608 + rows * 12_288, transcendentals=0
        ),
        name="project",
    )(order, mine, theirs, w, base)


def swap(array):
    return lax.ppermute(array, "c", [(0, 1), (1, 0)])


def ring(array, step):
    return lax.ppermute(array, "y", [(i, (i + step) % 4) for i in range(4)])


def in_three(array):
    parts = []
    for _ in range(3):
        part = lax.reduce_precision(array, 8, 7)
        parts.append(part.astype(jnp.bfloat16))
        array = array - part
    return parts


def shards(
    residual,
    queries,
    keys,
    values,
    documents,
    out_proj,
    modality,
    norm_gain,
    picks,
    router,
    w_gate,
    w_up,
    w_down,
):
    z, x, y, c = (lax.axis_index(name) for name in ALL)
    seq = z * 4 + x
    expert = y * 2 + c
    b = jnp.where(c == 0, x, z)

    got = exchange(pack_heads(queries, keys, values), GROUP_A)
    received = exchange(pack_parts(got), GROUP_B).reshape(BLOCKS, 1152, HD)

    index = jnp.arange(BLOCKS, dtype=jnp.int32)
    swapped = (index % 4) * 4 + index // 4
    bound = documents.shape[0] - jnp.sum(documents)
    tab = jnp.concatenate(
        [
            jnp.where(c == 0, swapped, index),
            jnp.where(c == 0, index, swapped),
            jnp.stack([bound, b]).astype(jnp.int32),
        ]
    ).astype(jnp.int32)
    attended = exchange(attend(tab, received), GROUP_AB)
    attended = attended.reshape(4, TOK, HD).transpose(1, 0, 2).reshape(TOK, 4 * HD)

    ranked = picks.reshape(8, 8, 16)
    inside = (ranked // TOK) == seq
    local = jnp.sum(jnp.where(inside, ranked - seq * TOK, 0), axis=1).T.reshape(128, 1)
    filled = jnp.any(inside, axis=1).T.reshape(128, 1)
    hot = ((jnp.arange(TOK, dtype=jnp.int32)[None, :] == local) & filled).astype(jnp.bfloat16)

    early = jnp.dot(hot, attended, preferred_element_type=jnp.float32).astype(jnp.bfloat16)
    gain_sent = jnp.stack(in_three(norm_gain), axis=1).reshape(12, 512)
    gain_sent = jnp.pad(gain_sent, ((0, 4), (0, 0)))
    early = jnp.concatenate([early, gain_sent], axis=0)
    mine = lax.all_to_all(jnp.broadcast_to(early[None], (4, 144, 512)), "y", 0, 0, tiled=True)
    theirs = swap(mine)
    chip = jnp.arange(4, dtype=jnp.int32)
    order = jnp.concatenate([2 * chip + c, 2 * chip + 1 - c]).astype(jnp.int32)
    base = jnp.dot(hot, residual, preferred_element_type=jnp.float32).astype(jnp.bfloat16)
    rows = project(order, mine, theirs, out_proj, base)
    gains = jnp.stack([mine[:, 128:140], theirs[:, 128:140]]).reshape(2, 4, 2, 3, 1024)
    gains = jnp.where(expert < 4, gains[:, :, 0], gains[:, :, 1]).astype(jnp.float32)
    gains = gains[:, :, 0] + (gains[:, :, 1] + gains[:, :, 2])
    gains = jnp.where(c == 0, gains, gains[::-1])
    gain = gains.transpose(1, 0, 2).reshape(1, D)

    held, rows = lax.optimization_barrier((attended, rows))
    arrived = lax.all_to_all(rows.reshape(128, 8, 128), ALL, 0, 0, tiled=True)
    before = ring(held, 1)
    after = ring(held, -1)
    half = TOK // 2
    opposite = jnp.concatenate([ring(before[:half], 1), ring(after[half:], -1)], axis=0)
    mine = jnp.stack([held, before, after, opposite])
    theirs = swap(mine)
    chip = jnp.remainder(y + jnp.array([0, 3, 1, 2], jnp.int32), 4)
    order = jnp.concatenate([2 * chip + c, 2 * chip + 1 - c]).astype(jnp.int32)
    hidden = project(order, mine, theirs, out_proj, residual)

    own = lax.dynamic_index_in_dim(ranked, expert, 0, keepdims=False)
    own = lax.dynamic_index_in_dim(own, seq, 1, keepdims=False)
    source = (own // TOK)[:, None] == jnp.arange(16, dtype=jnp.int32)[None, :]
    source = source.astype(jnp.bfloat16)
    taken = jnp.dot(source, arrived.reshape(16, D), preferred_element_type=jnp.float32)
    inverse = lax.rsqrt(jnp.mean(taken * taken, axis=1, keepdims=True) + 1e-05)
    chosen = (taken * inverse * gain).astype(jnp.bfloat16)
    logits = jnp.dot(chosen, router, preferred_element_type=jnp.float32)
    near = spread(chosen, GROUP_A)
    far = spread(near.reshape(32, D), GROUP_B)
    piece = far.reshape(128, D)
    gate_part = jnp.dot(piece, w_gate[0], preferred_element_type=jnp.float32)
    up_part = jnp.dot(piece, w_up[0], preferred_element_type=jnp.float32)
    inner_act = (jax.nn.silu(gate_part) * up_part).astype(jnp.bfloat16)
    partial = jnp.dot(inner_act, w_down[0], preferred_element_type=jnp.float32)
    partial = exchange(partial.astype(jnp.bfloat16).reshape(4, 32, D), GROUP_B)
    partial = jnp.sum(partial.astype(jnp.float32), axis=0).astype(jnp.bfloat16)
    partial = exchange(partial.reshape(4, 8, D), GROUP_A)
    summed = jnp.sum(partial.astype(jnp.float32), axis=0)
    weighted = (jax.nn.sigmoid(logits) * summed).astype(jnp.bfloat16)
    back = lax.dot_general(
        source, weighted, (((0,), (0,)), ((), ())), preferred_element_type=jnp.float32
    ).astype(jnp.bfloat16)
    returned = lax.all_to_all(back.reshape(128, 8, 128), ALL, 0, 0, tiled=True)
    expert_add = lax.dot_general(
        hot, returned.reshape(128, 1024), (((0,), (0,)), ((), ())), preferred_element_type=jnp.float32
    )
    return (hidden.astype(jnp.float32) + expert_add).astype(jnp.bfloat16)


def solution(mesh):
    finer = Mesh(mesh.devices.reshape(4, 4, 4, 2), ALL)
    in_specs = (
        P(SEQ, EXP),
        P(SEQ, EXP),
        P(SEQ, EXP),
        P(SEQ, EXP),
        P(),
        P(None, EXP),
        P(SEQ),
        P(None, EXP),
        P(),
        P(None, EXP),
        P(EXP, None, SEQ),
        P(EXP, None, SEQ),
        P(EXP, SEQ, None),
    )
    return jax.shard_map(
        shards, mesh=finer, in_specs=in_specs, out_specs=P(SEQ, EXP), check_vma=False
    )
```

```python
import functools
import math

import jax
import jax.numpy as jnp
import numpy as np
from jax import lax
from jax.experimental import pallas as pl
from jax.experimental.pallas import tpu as pltpu
from jax.sharding import Mesh
from jax.sharding import PartitionSpec as P

D = 8192
HD = 128
TOK = 512
BLOCKS = 16
ROOM = 56 << 20
ALL = ("z", "x", "y", "c")
SEQ = ("z", "x")
EXP = ("y", "c")
NEG = -1e30
SCALE = math.log2(math.e) / math.sqrt(HD)

IDS = np.arange(128).reshape(4, 4, 4, 2)


def _groups(first):
    rows = []
    for y in range(4):
        for k in range(4):
            along_z, along_x = IDS[:, k, y, :], IDS[k, :, y, :]
            rows.append([int(i) for i in (along_z if first else along_x)[:, 0]])
            rows.append([int(i) for i in (along_x if first else along_z)[:, 1]])
    return rows


def _group16():
    rows = []
    for y in range(4):
        rows.append([int(i) for i in IDS[:, :, y, 0].reshape(-1)])
        rows.append([int(i) for i in IDS[:, :, y, 1].T.reshape(-1)])
    return rows


GROUP_A = _groups(True)
GROUP_B = _groups(False)
GROUP_AB = _group16()


def exchange(array, groups):
    return lax.all_to_all(array, ALL, 0, 0, tiled=True, axis_index_groups=groups)


def spread(array, groups):
    return exchange(jnp.broadcast_to(array[None], (4, *array.shape)), groups)


def pack_heads_kernel(q, k, v, o):
    for h in range(4):
        for i, ref in enumerate((q, k, v)):
            o[h, i] = ref[:, h * HD : (h + 1) * HD]


def pack_heads(queries, keys, values):
    return pl.pallas_call(
        pack_heads_kernel,
        out_shape=jax.ShapeDtypeStruct((4, 3, TOK, HD), jnp.bfloat16),
        compiler_params=pltpu.CompilerParams(vmem_limit_bytes=ROOM),
        name="pack_heads",
    )(queries, keys, values)


def pack_parts_kernel(got, q, one, two):
    for i in range(2):
        one[0, i, 0:TOK] = got[i, 1]
        one[0, i, TOK : 2 * TOK] = got[i, 2]
        one[0, i, 2 * TOK : 2 * TOK + 128] = q[i, 0]
        one[0, i, 2 * TOK + 128 :] = q[i + 2, 0]
        two[0, i, 0:TOK] = got[i + 2, 1]
        two[0, i, TOK:] = got[i + 2, 2]


def pack_parts(got):
    return pl.pallas_call(
        pack_parts_kernel,
        grid=(4,),
        in_specs=[
            pl.BlockSpec((4, 3, TOK, HD), lambda p: (0, 0, 0, 0)),
            pl.BlockSpec((4, 1, 128, HD), lambda p: (0, 0, p, 0)),
        ],
        out_specs=[
            pl.BlockSpec((1, 2, 1280, HD), lambda p: (p, 0, 0, 0)),
            pl.BlockSpec((1, 2, 1024, HD), lambda p: (p, 0, 0, 0)),
        ],
        out_shape=[
            jax.ShapeDtypeStruct((4, 2, 1280, HD), jnp.bfloat16),
            jax.ShapeDtypeStruct((4, 2, 1024, HD), jnp.bfloat16),
        ],
        compiler_params=pltpu.CompilerParams(vmem_limit_bytes=20 << 20),
        name="pack_parts",
    )(got, got)


QW = 512
TILE = QW // 128
TILES = BLOCKS // TILE


def attend_kernel(tab, r, *refs, part):
    if part == 0:
        mo, lo_, acco, qto, vt, s0, s1, acc, m, l = refs
    else:
        mi, li, acci, qti, o, vt, s0, s1, acc, m, l = refs
    bound, sub, core = tab[48], tab[49], tab[50]
    start = jnp.where(core == 0, 4 * part, part)

    def turn(t, carry):
        vt[t] = r[t, TOK : 2 * TOK, :].T
        return carry

    lax.fori_loop(0, 8, turn, 0)
    col = lax.broadcasted_iota(jnp.int32, (1, QW), 1)
    row = lax.broadcasted_iota(jnp.int32, (TOK, 1), 0)

    def tile(index, carry):
        j = TILE * index
        if part == 0:
            qt = qto.at[index]
            for i in range(TILE):
                here = r[tab[j + i], pl.ds(2 * TOK + 128 * tab[32 + j + i], 128), :]
                qt[:, i * 128 : (i + 1) * 128] = here.T
            m[...] = jnp.full((1, QW), NEG, jnp.float32)
            l[...] = jnp.zeros((1, QW), jnp.float32)
            acc[...] = jnp.zeros((HD, QW), jnp.float32)
        else:
            qt = qti.at[index]
            m[...] = mi[index]
            l[...] = li[index]
            acc[...] = acci[index]
        first = j * TOK + sub * 128
        last = first + (TILE - 1) * TOK + 127
        qpos = first + (col // 128) * TOK + col % 128
        qlow = jnp.where(qpos >= bound, bound, 0)
        lo = jnp.where(first >= bound, bound // (2 * TOK), 0)
        hi = (j + TILE) // 2
        lo = (jnp.maximum(lo - start, 0) + core) >> core
        hi = jnp.minimum((jnp.maximum(hi - start, 0) + core) >> core, 4)

        def score(t):
            return jnp.dot(r[tab[t], 0:TOK, :], qt[...], preferred_element_type=jnp.float32)

        def soft(s, t, masked):
            here = s[...]
            if masked:
                kpos = t * TOK + row
                here = jnp.where((kpos <= qpos) & (kpos >= qlow), here, NEG)
            old = m[...]
            new = jnp.maximum(old, jnp.max(here, axis=0, keepdims=True))
            p = jnp.exp2(here * SCALE - new * SCALE)
            f = jnp.exp2((old - new) * SCALE)
            m[...] = new
            l[...] = l[...] * f + jnp.sum(p, axis=0, keepdims=True)
            acc[...] = acc[...] * f + jnp.dot(
                vt[tab[t]], p.astype(jnp.bfloat16), preferred_element_type=jnp.float32
            )

        def first_of(i):
            return 2 * (start + (i << core))

        s0[...] = score(first_of(jnp.minimum(lo, 3)))

        def step(i, inner):
            t = first_of(i)

            def go(masked):
                s1[...] = score(t + 1)
                soft(s0, t, masked)
                s0[...] = score(first_of(jnp.minimum(i + 1, 3)))
                soft(s1, t + 1, masked)

            need = ((t + 2) * TOK - 1 > first) | ((t * TOK < bound) & (last >= bound))
            pl.when(need)(lambda: go(True))
            pl.when(jnp.logical_not(need))(lambda: go(False))
            return inner

        lax.fori_loop(lo, hi, step, 0)
        if part == 0:
            mo[index] = m[...]
            lo_[index] = l[...]
            acco[index] = acc[...]
        else:
            out = (acc[...] / l[...]).T.astype(jnp.bfloat16)
            for i in range(TILE):
                o[tab[16 + j + i]] = out[i * 128 : (i + 1) * 128]
        return carry

    lax.fori_loop(0, TILES, tile, 0)


def attend(part, tab, received, *state):
    vmem = pl.BlockSpec(memory_space=pltpu.VMEM)
    if part == 0:
        out_shape = [
            jax.ShapeDtypeStruct((TILES, 1, QW), jnp.float32),
            jax.ShapeDtypeStruct((TILES, 1, QW), jnp.float32),
            jax.ShapeDtypeStruct((TILES, HD, QW), jnp.float32),
            jax.ShapeDtypeStruct((TILES, HD, QW), jnp.bfloat16),
        ]
    else:
        out_shape = jax.ShapeDtypeStruct((BLOCKS, 128, HD), jnp.bfloat16)
    return pl.pallas_call(
        functools.partial(attend_kernel, part=part),
        out_shape=out_shape,
        in_specs=[pl.BlockSpec(memory_space=pltpu.SMEM), vmem] + [vmem] * len(state),
        out_specs=[vmem] * 4 if part == 0 else vmem,
        scratch_shapes=[
            pltpu.VMEM((8, HD, TOK), jnp.bfloat16),
            pltpu.VMEM((TOK, QW), jnp.float32),
            pltpu.VMEM((TOK, QW), jnp.float32),
            pltpu.VMEM((HD, QW), jnp.float32),
            pltpu.VMEM((1, QW), jnp.float32),
            pltpu.VMEM((1, QW), jnp.float32),
        ],
        compiler_params=pltpu.CompilerParams(vmem_limit_bytes=24 << 20),
        cost_estimate=pl.CostEstimate(
            flops=6_000_000_000, bytes_accessed=4_000_000, transcendentals=4_000_000
        ),
        name="attend",
    )(tab, received, *state)


def project_kernel(order, mine, theirs, w, base, o, xs, ws, acc, sem):
    copies = []
    for k in range(8):
        part = (mine if k < 4 else theirs).at[k % 4, pl.ds(0, xs.shape[1])]
        rows = pl.ds(pl.multiple_of(order[k] * 512, 512), 512)
        copies.append(
            (
                pltpu.make_async_copy(part, xs.at[k], sem.at[0, k]),
                pltpu.make_async_copy(w.at[rows], ws.at[k], sem.at[1, k]),
            )
        )
        for copy in copies[-1]:
            copy.start()
    for k in range(8):
        for copy in copies[k]:
            copy.wait()
        term = jnp.dot(xs[k], ws[k], preferred_element_type=jnp.float32)
        if k == 0:
            acc[...] = base[...].astype(jnp.float32) + term
        elif k < 7:
            acc[...] += term
        else:
            o[...] = (acc[...] + term).astype(jnp.bfloat16)


def project(order, mine, theirs, w, base):
    rows = base.shape[0]
    vmem, anywhere = pl.BlockSpec(memory_space=pltpu.VMEM), pl.BlockSpec(memory_space=pl.ANY)
    return pl.pallas_call(
        project_kernel,
        in_specs=[pl.BlockSpec(memory_space=pltpu.SMEM), anywhere, anywhere, anywhere, vmem],
        out_specs=vmem,
        out_shape=jax.ShapeDtypeStruct((rows, 1024), jnp.bfloat16),
        scratch_shapes=[
            pltpu.VMEM((8, rows, 512), jnp.bfloat16),
            pltpu.VMEM((8, 512, 1024), jnp.bfloat16),
            pltpu.VMEM((rows, 1024), jnp.float32),
            pltpu.SemaphoreType.DMA((2, 8)),
        ],
        compiler_params=pltpu.CompilerParams(vmem_limit_bytes=ROOM),
        cost_estimate=pl.CostEstimate(
            flops=rows * 8_388_608, bytes_accessed=8_388_608 + rows * 12_288, transcendentals=0
        ),
        name="project",
    )(order, mine, theirs, w, base)


def experts_kernel(piece, gate, up, down, o, ps, gs, us, ds, sem):
    wide = D // 4
    copies = []
    for k in range(4):
        span = pl.ds(k * wide, wide)
        copies.append(
            (
                pltpu.make_async_copy(piece.at[:, span], ps.at[k], sem.at[0, k]),
                pltpu.make_async_copy(gate.at[0, span], gs.at[k], sem.at[1, k]),
                pltpu.make_async_copy(up.at[0, span], us.at[k], sem.at[2, k]),
            )
        )
    last = [
        pltpu.make_async_copy(down.at[0, :, pl.ds(k * wide, wide)], ds.at[k], sem.at[3, k])
        for k in range(4)
    ]
    for group in (*copies, last):
        for copy in group:
            copy.start()
    g = u = None
    for k in range(4):
        for copy in copies[k]:
            copy.wait()
        add_g = jnp.dot(ps[k], gs[k], preferred_element_type=jnp.float32)
        add_u = jnp.dot(ps[k], us[k], preferred_element_type=jnp.float32)
        g, u = (add_g, add_u) if k == 0 else (g + add_g, u + add_u)
    inner = (jax.nn.silu(g) * u).astype(jnp.bfloat16)
    for k in range(4):
        last[k].wait()
        o[:, k * wide : (k + 1) * wide] = jnp.dot(
            inner, ds[k], preferred_element_type=jnp.float32
        ).astype(o.dtype)


def experts(piece, w_gate, w_up, w_down):
    anywhere = pl.BlockSpec(memory_space=pl.ANY)
    return pl.pallas_call(
        experts_kernel,
        in_specs=[anywhere] * 4,
        out_specs=pl.BlockSpec(memory_space=pltpu.VMEM),
        out_shape=jax.ShapeDtypeStruct((128, D), jnp.bfloat16),
        scratch_shapes=[
            pltpu.VMEM((4, 128, D // 4), jnp.bfloat16),
            pltpu.VMEM((4, D // 4, 256), jnp.bfloat16),
            pltpu.VMEM((4, D // 4, 256), jnp.bfloat16),
            pltpu.VMEM((4, 256, D // 4), jnp.bfloat16),
            pltpu.SemaphoreType.DMA((4, 4)),
        ],
        compiler_params=pltpu.CompilerParams(vmem_limit_bytes=ROOM),
        cost_estimate=pl.CostEstimate(
            flops=1_610_000_000, bytes_accessed=16_800_000, transcendentals=32_768
        ),
        name="experts",
    )(piece, w_gate, w_up, w_down)


def swap(array):
    return lax.ppermute(array, "c", [(0, 1), (1, 0)])


def ring(array, step):
    return lax.ppermute(array, "y", [(i, (i + step) % 4) for i in range(4)])


def in_three(array):
    parts = []
    for _ in range(3):
        part = lax.reduce_precision(array, 8, 7)
        parts.append(part.astype(jnp.bfloat16))
        array = array - part
    return parts


def shards(
    residual,
    queries,
    keys,
    values,
    documents,
    out_proj,
    modality,
    norm_gain,
    picks,
    router,
    w_gate,
    w_up,
    w_down,
):
    z, x, y, c = (lax.axis_index(name) for name in ALL)
    seq = z * 4 + x
    expert = y * 2 + c
    b = jnp.where(c == 0, x, z)

    got = exchange(pack_heads(queries, keys, values), GROUP_A)
    one, two = pack_parts(got)
    one = exchange(one, GROUP_B).reshape(8, 1280, HD)
    one, two = lax.optimization_barrier((one, two))
    two = exchange(two, GROUP_B).reshape(8, 1024, HD)

    index = jnp.arange(BLOCKS, dtype=jnp.int32)
    low, high = index % 4, index // 4
    from_a = jnp.where(c == 0, high, low)
    from_b = jnp.where(c == 0, low, high)
    bound = documents.shape[0] - jnp.sum(documents)
    tab = jnp.concatenate(
        [
            from_b * 2 + from_a % 2,
            from_a * 4 + from_b,
            from_a // 2,
            jnp.stack([bound, b, c]).astype(jnp.int32),
        ]
    ).astype(jnp.int32)
    state = attend(0, tab, one)
    attended = attend(1, tab, two, *state)
    attended = exchange(attended, GROUP_AB)
    attended = attended.reshape(4, TOK, HD).transpose(1, 0, 2).reshape(TOK, 4 * HD)

    ranked = picks.reshape(8, 8, 16)
    inside = (ranked // TOK) == seq
    local = jnp.sum(jnp.where(inside, ranked - seq * TOK, 0), axis=1).T.reshape(128, 1)
    filled = jnp.any(inside, axis=1).T.reshape(128, 1)
    hot = ((jnp.arange(TOK, dtype=jnp.int32)[None, :] == local) & filled).astype(jnp.bfloat16)

    early = jnp.dot(hot, attended, preferred_element_type=jnp.float32).astype(jnp.bfloat16)
    gain_sent = jnp.stack(in_three(norm_gain), axis=1).reshape(12, 512)
    gain_sent = jnp.pad(gain_sent, ((0, 4), (0, 0)))
    early = jnp.concatenate([early, gain_sent], axis=0)
    mine = lax.all_to_all(jnp.broadcast_to(early[None], (4, 144, 512)), "y", 0, 0, tiled=True)
    theirs = swap(mine)
    chip = jnp.arange(4, dtype=jnp.int32)
    order = jnp.concatenate([2 * chip + c, 2 * chip + 1 - c]).astype(jnp.int32)
    base = jnp.dot(hot, residual, preferred_element_type=jnp.float32).astype(jnp.bfloat16)
    rows = project(order, mine, theirs, out_proj, base)
    gains = jnp.stack([mine[:, 128:140], theirs[:, 128:140]]).reshape(2, 4, 2, 3, 1024)
    gains = jnp.where(expert < 4, gains[:, :, 0], gains[:, :, 1]).astype(jnp.float32)
    gains = gains[:, :, 0] + (gains[:, :, 1] + gains[:, :, 2])
    gains = jnp.where(c == 0, gains, gains[::-1])
    gain = gains.transpose(1, 0, 2).reshape(1, D)

    held, rows = lax.optimization_barrier((attended, rows))
    arrived = lax.all_to_all(rows.reshape(128, 8, 128), ALL, 0, 0, tiled=True)
    before = ring(held, 1)
    after = ring(held, -1)
    half = TOK // 2
    opposite = jnp.concatenate([ring(before[:half], 1), ring(after[half:], -1)], axis=0)
    mine = jnp.stack([held, before, after, opposite])
    theirs = swap(mine)
    chip = jnp.remainder(y + jnp.array([0, 3, 1, 2], jnp.int32), 4)
    order = jnp.concatenate([2 * chip + c, 2 * chip + 1 - c]).astype(jnp.int32)
    hidden = project(order, mine, theirs, out_proj, residual)

    own = lax.dynamic_index_in_dim(ranked, expert, 0, keepdims=False)
    own = lax.dynamic_index_in_dim(own, seq, 1, keepdims=False)
    source = (own // TOK)[:, None] == jnp.arange(16, dtype=jnp.int32)[None, :]
    source = source.astype(jnp.bfloat16)
    taken = jnp.dot(source, arrived.reshape(16, D), preferred_element_type=jnp.float32)
    inverse = lax.rsqrt(jnp.mean(taken * taken, axis=1, keepdims=True) + 1e-05)
    chosen = (taken * inverse * gain).astype(jnp.bfloat16)
    logits = jnp.dot(chosen, router, preferred_element_type=jnp.float32)
    near = spread(chosen, GROUP_A)
    far = spread(near.reshape(32, D), GROUP_B)
    piece = far.reshape(128, D)
    partial = experts(piece, w_gate, w_up, w_down)
    partial = exchange(partial.reshape(4, 32, D), GROUP_B)
    partial = jnp.sum(partial.astype(jnp.float32), axis=0).astype(jnp.bfloat16)
    partial = exchange(partial.reshape(4, 8, D), GROUP_A)
    summed = jnp.sum(partial.astype(jnp.float32), axis=0)
    weighted = (jax.nn.sigmoid(logits) * summed).astype(jnp.bfloat16)
    back = lax.dot_general(
        source, weighted, (((0,), (0,)), ((), ())), preferred_element_type=jnp.float32
    ).astype(jnp.bfloat16)
    returned = lax.all_to_all(back.reshape(128, 8, 128), ALL, 0, 0, tiled=True)
    expert_add = lax.dot_general(
        hot, returned.reshape(128, 1024), (((0,), (0,)), ((), ())), preferred_element_type=jnp.float32
    )
    return (hidden.astype(jnp.float32) + expert_add).astype(jnp.bfloat16)


def solution(mesh):
    finer = Mesh(mesh.devices.reshape(4, 4, 4, 2), ALL)
    in_specs = (
        P(SEQ, EXP),
        P(SEQ, EXP),
        P(SEQ, EXP),
        P(SEQ, EXP),
        P(),
        P(None, EXP),
        P(SEQ),
        P(None, EXP),
        P(),
        P(None, EXP),
        P(EXP, None, SEQ),
        P(EXP, None, SEQ),
        P(EXP, SEQ, None),
    )
    return jax.shard_map(
        shards, mesh=finer, in_specs=in_specs, out_specs=P(SEQ, EXP), check_vma=False
    )
```

```python
import functools
import math

import jax
import jax.numpy as jnp
import numpy as np
from jax import lax
from jax.experimental import pallas as pl
from jax.experimental.pallas import tpu as pltpu
from jax.sharding import Mesh
from jax.sharding import PartitionSpec as P

D = 8192
HD = 128
TOK = 512
BLOCKS = 16
ROOM = 50 << 20
ALL = ("z", "x", "y", "c")
SEQ = ("z", "x")
EXP = ("y", "c")
NEG = -1e30
SCALE = math.log2(math.e) / math.sqrt(HD)

IDS = np.arange(128).reshape(4, 4, 4, 2)


def _groups(first):
    rows = []
    for y in range(4):
        for k in range(4):
            along_z, along_x = IDS[:, k, y, :], IDS[k, :, y, :]
            rows.append([int(i) for i in (along_z if first else along_x)[:, 0]])
            rows.append([int(i) for i in (along_x if first else along_z)[:, 1]])
    return rows


def _group16():
    rows = []
    for y in range(4):
        rows.append([int(i) for i in IDS[:, :, y, 0].reshape(-1)])
        rows.append([int(i) for i in IDS[:, :, y, 1].T.reshape(-1)])
    return rows


GROUP_A = _groups(True)
GROUP_B = _groups(False)
GROUP_AB = _group16()


def exchange(array, groups):
    return lax.all_to_all(array, ALL, 0, 0, tiled=True, axis_index_groups=groups)


def spread(array, groups):
    return exchange(jnp.broadcast_to(array[None], (4, *array.shape)), groups)


def pack_heads_kernel(q, k, v, o):
    for h in range(4):
        for i, ref in enumerate((q, k, v)):
            o[h, i] = ref[:, h * HD : (h + 1) * HD]


def pack_heads(queries, keys, values):
    return pl.pallas_call(
        pack_heads_kernel,
        out_shape=jax.ShapeDtypeStruct((4, 3, TOK, HD), jnp.bfloat16),
        compiler_params=pltpu.CompilerParams(vmem_limit_bytes=ROOM),
        name="pack_heads",
    )(queries, keys, values)


def pack_parts_kernel(got, q, one, two):
    for i in range(2):
        one[0, i, 0:TOK] = got[i, 1]
        one[0, i, TOK : 2 * TOK] = got[i, 2]
        one[0, i, 2 * TOK : 2 * TOK + 128] = q[i, 0]
        one[0, i, 2 * TOK + 128 :] = q[i + 2, 0]
        two[0, i, 0:TOK] = got[i + 2, 1]
        two[0, i, TOK:] = got[i + 2, 2]


def pack_parts(got):
    return pl.pallas_call(
        pack_parts_kernel,
        grid=(4,),
        in_specs=[
            pl.BlockSpec((4, 3, TOK, HD), lambda p: (0, 0, 0, 0)),
            pl.BlockSpec((4, 1, 128, HD), lambda p: (0, 0, p, 0)),
        ],
        out_specs=[
            pl.BlockSpec((1, 2, 1280, HD), lambda p: (p, 0, 0, 0)),
            pl.BlockSpec((1, 2, 1024, HD), lambda p: (p, 0, 0, 0)),
        ],
        out_shape=[
            jax.ShapeDtypeStruct((4, 2, 1280, HD), jnp.bfloat16),
            jax.ShapeDtypeStruct((4, 2, 1024, HD), jnp.bfloat16),
        ],
        compiler_params=pltpu.CompilerParams(vmem_limit_bytes=20 << 20),
        name="pack_parts",
    )(got, got)


QW = 512
TILE = QW // 128
TILES = BLOCKS // TILE


def attend_kernel(tab, r, *refs, part):
    if part == 0:
        mo, lo_, acco, qto, vt, s0, s1, acc, m, l = refs
    else:
        mi, li, acci, qti, o, vt, s0, s1, acc, m, l = refs
    bound, sub, core = tab[48], tab[49], tab[50]
    start = jnp.where(core == 0, 4 * part, part)

    def turn(t, carry):
        vt[t] = r[t, TOK : 2 * TOK, :].T
        return carry

    lax.fori_loop(0, 8, turn, 0)
    col = lax.broadcasted_iota(jnp.int32, (1, QW), 1)
    row = lax.broadcasted_iota(jnp.int32, (TOK, 1), 0)

    def tile(index, carry):
        j = TILE * index
        if part == 0:
            qt = qto.at[index]
            for i in range(TILE):
                here = r[tab[j + i], pl.ds(2 * TOK + 128 * tab[32 + j + i], 128), :]
                qt[:, i * 128 : (i + 1) * 128] = here.T
            m[...] = jnp.full((1, QW), NEG, jnp.float32)
            l[...] = jnp.zeros((1, QW), jnp.float32)
            acc[...] = jnp.zeros((HD, QW), jnp.float32)
        else:
            qt = qti.at[index]
            m[...] = mi[index]
            l[...] = li[index]
            acc[...] = acci[index]
        first = j * TOK + sub * 128
        last = first + (TILE - 1) * TOK + 127
        qpos = first + (col // 128) * TOK + col % 128
        qlow = jnp.where(qpos >= bound, bound, 0)
        lo = jnp.where(first >= bound, bound // (2 * TOK), 0)
        hi = (j + TILE) // 2
        lo = (jnp.maximum(lo - start, 0) + core) >> core
        hi = jnp.minimum((jnp.maximum(hi - start, 0) + core) >> core, 4)

        def score(t):
            return jnp.dot(r[tab[t], 0:TOK, :], qt[...], preferred_element_type=jnp.float32)

        def soft(s, t, masked):
            here = s[...]
            if masked:
                kpos = t * TOK + row
                here = jnp.where((kpos <= qpos) & (kpos >= qlow), here, NEG)
            old = m[...]
            new = jnp.maximum(old, jnp.max(here, axis=0, keepdims=True))
            p = jnp.exp2(here * SCALE - new * SCALE)
            f = jnp.exp2((old - new) * SCALE)
            m[...] = new
            l[...] = l[...] * f + jnp.sum(p, axis=0, keepdims=True)
            acc[...] = acc[...] * f + jnp.dot(
                vt[tab[t]], p.astype(jnp.bfloat16), preferred_element_type=jnp.float32
            )

        def first_of(i):
            return 2 * (start + (i << core))

        s0[...] = score(first_of(jnp.minimum(lo, 3)))

        def step(i, inner):
            t = first_of(i)

            def go(masked):
                s1[...] = score(t + 1)
                soft(s0, t, masked)
                s0[...] = score(first_of(jnp.minimum(i + 1, 3)))
                soft(s1, t + 1, masked)

            need = ((t + 2) * TOK - 1 > first) | ((t * TOK < bound) & (last >= bound))
            pl.when(need)(lambda: go(True))
            pl.when(jnp.logical_not(need))(lambda: go(False))
            return inner

        lax.fori_loop(lo, hi, step, 0)
        if part == 0:
            mo[index] = m[...]
            lo_[index] = l[...]
            acco[index] = acc[...]
        else:
            out = (acc[...] / l[...]).T.astype(jnp.bfloat16)
            for i in range(TILE):
                o[tab[16 + j + i]] = out[i * 128 : (i + 1) * 128]
        return carry

    lax.fori_loop(0, TILES, tile, 0)


def attend(part, tab, received, *state):
    vmem = pl.BlockSpec(memory_space=pltpu.VMEM)
    if part == 0:
        out_shape = [
            jax.ShapeDtypeStruct((TILES, 1, QW), jnp.float32),
            jax.ShapeDtypeStruct((TILES, 1, QW), jnp.float32),
            jax.ShapeDtypeStruct((TILES, HD, QW), jnp.float32),
            jax.ShapeDtypeStruct((TILES, HD, QW), jnp.bfloat16),
        ]
    else:
        out_shape = jax.ShapeDtypeStruct((BLOCKS, 128, HD), jnp.bfloat16)
    return pl.pallas_call(
        functools.partial(attend_kernel, part=part),
        out_shape=out_shape,
        in_specs=[pl.BlockSpec(memory_space=pltpu.SMEM), vmem] + [vmem] * len(state),
        out_specs=[vmem] * 4 if part == 0 else vmem,
        scratch_shapes=[
            pltpu.VMEM((8, HD, TOK), jnp.bfloat16),
            pltpu.VMEM((TOK, QW), jnp.float32),
            pltpu.VMEM((TOK, QW), jnp.float32),
            pltpu.VMEM((HD, QW), jnp.float32),
            pltpu.VMEM((1, QW), jnp.float32),
            pltpu.VMEM((1, QW), jnp.float32),
        ],
        compiler_params=pltpu.CompilerParams(vmem_limit_bytes=24 << 20),
        cost_estimate=pl.CostEstimate(
            flops=6_000_000_000, bytes_accessed=4_000_000, transcendentals=4_000_000
        ),
        name="attend",
    )(tab, received, *state)


def project_kernel(order, mine, theirs, w, base, o, ws, acc, sem):
    copies = []
    for k in range(8):
        rows = pl.ds(pl.multiple_of(order[k] * 512, 512), 512)
        copies.append(pltpu.make_async_copy(w.at[rows], ws.at[k], sem.at[k]))
        copies[-1].start()
    for k in range(8):
        part = (mine if k < 4 else theirs)[k % 4, 0 : acc.shape[0]]
        copies[k].wait()
        term = jnp.dot(part, ws[k], preferred_element_type=jnp.float32)
        if k == 0:
            acc[...] = base[...].astype(jnp.float32) + term
        elif k < 7:
            acc[...] += term
        else:
            total = (acc[...] + term).astype(jnp.bfloat16)
            o[...] = total.reshape(o.shape)


def project(order, mine, theirs, w, base, shape):
    rows = base.shape[0]
    vmem = pl.BlockSpec(memory_space=pltpu.VMEM)
    hbm = pl.BlockSpec(memory_space=pltpu.HBM)
    return pl.pallas_call(
        project_kernel,
        in_specs=[pl.BlockSpec(memory_space=pltpu.SMEM), vmem, vmem, hbm, vmem],
        out_specs=vmem,
        out_shape=jax.ShapeDtypeStruct(shape, jnp.bfloat16),
        scratch_shapes=[
            pltpu.VMEM((8, 512, 1024), jnp.bfloat16),
            pltpu.VMEM((rows, 1024), jnp.float32),
            pltpu.SemaphoreType.DMA((8,)),
        ],
        compiler_params=pltpu.CompilerParams(vmem_limit_bytes=ROOM),
        cost_estimate=pl.CostEstimate(
            flops=rows * 8_388_608, bytes_accessed=8_388_608 + rows * 12_288, transcendentals=0
        ),
        name="project",
    )(order, mine, theirs, w, base)


def experts_kernel(piece, gate, up, down, o, gs, us, ds, sem):
    wide = D // 4
    copies = []
    for k in range(4):
        span = pl.ds(k * wide, wide)
        copies.append(
            (
                pltpu.make_async_copy(gate.at[0, span], gs.at[k], sem.at[0, k]),
                pltpu.make_async_copy(up.at[0, span], us.at[k], sem.at[1, k]),
            )
        )
    last = [
        pltpu.make_async_copy(down.at[0, :, pl.ds(k * wide, wide)], ds.at[k], sem.at[2, k])
        for k in range(4)
    ]
    for group in (*copies, last):
        for copy in group:
            copy.start()
    g = u = None
    for k in range(4):
        for copy in copies[k]:
            copy.wait()
        rows = piece[:, k * wide : (k + 1) * wide]
        add_g = jnp.dot(rows, gs[k], preferred_element_type=jnp.float32)
        add_u = jnp.dot(rows, us[k], preferred_element_type=jnp.float32)
        g, u = (add_g, add_u) if k == 0 else (g + add_g, u + add_u)
    inner = (jax.nn.silu(g) * u).astype(jnp.bfloat16)
    for k in range(4):
        last[k].wait()
        o[:, k * wide : (k + 1) * wide] = jnp.dot(
            inner, ds[k], preferred_element_type=jnp.float32
        ).astype(o.dtype)


def experts(piece, w_gate, w_up, w_down):
    hbm = pl.BlockSpec(memory_space=pltpu.HBM)
    return pl.pallas_call(
        experts_kernel,
        in_specs=[pl.BlockSpec(memory_space=pltpu.VMEM)] + [hbm] * 3,
        out_specs=pl.BlockSpec(memory_space=pltpu.VMEM),
        out_shape=jax.ShapeDtypeStruct((128, D), jnp.bfloat16),
        scratch_shapes=[
            pltpu.VMEM((4, D // 4, 256), jnp.bfloat16),
            pltpu.VMEM((4, D // 4, 256), jnp.bfloat16),
            pltpu.VMEM((4, 256, D // 4), jnp.bfloat16),
            pltpu.SemaphoreType.DMA((3, 4)),
        ],
        compiler_params=pltpu.CompilerParams(vmem_limit_bytes=ROOM),
        cost_estimate=pl.CostEstimate(
            flops=1_610_000_000, bytes_accessed=16_800_000, transcendentals=32_768
        ),
        name="experts",
    )(piece, w_gate, w_up, w_down)


def swap(array):
    return lax.ppermute(array, "c", [(0, 1), (1, 0)])


def ring(array, step):
    return lax.ppermute(array, "y", [(i, (i + step) % 4) for i in range(4)])


def in_three(array):
    parts = []
    for _ in range(3):
        part = lax.reduce_precision(array, 8, 7)
        parts.append(part.astype(jnp.bfloat16))
        array = array - part
    return parts


def shards(
    residual,
    queries,
    keys,
    values,
    documents,
    out_proj,
    modality,
    norm_gain,
    picks,
    router,
    w_gate,
    w_up,
    w_down,
):
    z, x, y, c = (lax.axis_index(name) for name in ALL)
    seq = z * 4 + x
    expert = y * 2 + c
    b = jnp.where(c == 0, x, z)

    got = exchange(pack_heads(queries, keys, values), GROUP_A)
    one, two = pack_parts(got)
    one = exchange(one, GROUP_B).reshape(8, 1280, HD)
    one, two = lax.optimization_barrier((one, two))
    two = exchange(two, GROUP_B).reshape(8, 1024, HD)

    index = jnp.arange(BLOCKS, dtype=jnp.int32)
    low, high = index % 4, index // 4
    from_a = jnp.where(c == 0, high, low)
    from_b = jnp.where(c == 0, low, high)
    bound = documents.shape[0] - jnp.sum(documents)
    tab = jnp.concatenate(
        [
            from_b * 2 + from_a % 2,
            from_a * 4 + from_b,
            from_a // 2,
            jnp.stack([bound, b, c]).astype(jnp.int32),
        ]
    ).astype(jnp.int32)
    ranked = picks.reshape(8, 8, 16)
    inside = (ranked // TOK) == seq
    local = jnp.sum(jnp.where(inside, ranked - seq * TOK, 0), axis=1).T.reshape(128, 1)
    filled = jnp.any(inside, axis=1).T.reshape(128, 1)
    hot = ((jnp.arange(TOK, dtype=jnp.int32)[None, :] == local) & filled).astype(jnp.bfloat16)

    base = jnp.dot(hot, residual, preferred_element_type=jnp.float32).astype(jnp.bfloat16)
    gain_sent = jnp.stack(in_three(norm_gain), axis=1).reshape(12, 512)
    gain_sent = jnp.pad(gain_sent, ((0, 4), (0, 0)))

    state = attend(0, tab, one)
    attended = attend(1, tab, two, *state)
    attended = exchange(attended, GROUP_AB)
    attended, hot, base, gain_sent = lax.optimization_barrier((attended, hot, base, gain_sent))
    attended = attended.reshape(4, TOK, HD).transpose(1, 0, 2).reshape(TOK, 4 * HD)

    early = jnp.dot(hot, attended, preferred_element_type=jnp.float32).astype(jnp.bfloat16)
    early = jnp.concatenate([early, gain_sent], axis=0)
    mine = lax.all_to_all(jnp.broadcast_to(early[None], (4, 144, 512)), "y", 0, 0, tiled=True)
    theirs = swap(mine)
    chip = jnp.arange(4, dtype=jnp.int32)
    order = jnp.concatenate([2 * chip + c, 2 * chip + 1 - c]).astype(jnp.int32)
    rows = project(order, mine, theirs, out_proj, base, (128, 8, 128))
    gains = jnp.stack([mine[:, 128:140], theirs[:, 128:140]]).reshape(2, 4, 2, 3, 1024)
    gains = jnp.where(expert < 4, gains[:, :, 0], gains[:, :, 1]).astype(jnp.float32)
    gains = gains[:, :, 0] + (gains[:, :, 1] + gains[:, :, 2])
    gains = jnp.where(c == 0, gains, gains[::-1])
    gain = gains.transpose(1, 0, 2).reshape(1, D)

    held, rows = lax.optimization_barrier((attended, rows))
    arrived = lax.all_to_all(rows, ALL, 0, 0, tiled=True)
    before = ring(held, 1)
    after = ring(held, -1)
    half = TOK // 2
    opposite = jnp.concatenate([ring(before[:half], 1), ring(after[half:], -1)], axis=0)
    mine = jnp.stack([held, before, after, opposite])
    theirs = swap(mine)
    chip = jnp.remainder(y + jnp.array([0, 3, 1, 2], jnp.int32), 4)
    order = jnp.concatenate([2 * chip + c, 2 * chip + 1 - c]).astype(jnp.int32)
    own = lax.dynamic_index_in_dim(ranked, expert, 0, keepdims=False)
    own = lax.dynamic_index_in_dim(own, seq, 1, keepdims=False)
    source = (own // TOK)[:, None] == jnp.arange(16, dtype=jnp.int32)[None, :]
    source = source.astype(jnp.bfloat16)
    taken = jnp.dot(source, arrived.reshape(16, D), preferred_element_type=jnp.float32)
    inverse = lax.rsqrt(jnp.mean(taken * taken, axis=1, keepdims=True) + 1e-05)
    chosen = (taken * inverse * gain).astype(jnp.bfloat16)
    logits = jnp.dot(chosen, router, preferred_element_type=jnp.float32)
    near = spread(chosen, GROUP_A)
    far = spread(near.reshape(32, D), GROUP_B)
    piece = far.reshape(128, D)
    partial = experts(piece, w_gate, w_up, w_down)
    partial = exchange(partial.reshape(4, 32, D), GROUP_B)
    partial = jnp.sum(partial.astype(jnp.float32), axis=0).astype(jnp.bfloat16)
    partial = exchange(partial.reshape(4, 8, D), GROUP_A)
    summed = jnp.sum(partial.astype(jnp.float32), axis=0)
    weighted = (jax.nn.sigmoid(logits) * summed).astype(jnp.bfloat16)
    back = lax.dot_general(
        source, weighted, (((0,), (0,)), ((), ())), preferred_element_type=jnp.float32
    ).astype(jnp.bfloat16)
    back, mine, theirs = lax.optimization_barrier((back, mine, theirs))
    hidden = project(order, mine, theirs, out_proj, residual, (TOK, 1024))
    returned = lax.all_to_all(back.reshape(128, 8, 128), ALL, 0, 0, tiled=True)
    expert_add = lax.dot_general(
        hot, returned.reshape(128, 1024), (((0,), (0,)), ((), ())), preferred_element_type=jnp.float32
    )
    return (hidden.astype(jnp.float32) + expert_add).astype(jnp.bfloat16)


def solution(mesh):
    finer = Mesh(mesh.devices.reshape(4, 4, 4, 2), ALL)
    in_specs = (
        P(SEQ, EXP),
        P(SEQ, EXP),
        P(SEQ, EXP),
        P(SEQ, EXP),
        P(),
        P(None, EXP),
        P(SEQ),
        P(None, EXP),
        P(),
        P(None, EXP),
        P(EXP, None, SEQ),
        P(EXP, None, SEQ),
        P(EXP, SEQ, None),
    )
    return jax.shard_map(
        shards, mesh=finer, in_specs=in_specs, out_specs=P(SEQ, EXP), check_vma=False
    )
```

```python
import functools
import math

import jax
import jax.numpy as jnp
import numpy as np
from jax import lax
from jax.experimental import pallas as pl
from jax.experimental.pallas import tpu as pltpu
from jax.sharding import Mesh
from jax.sharding import PartitionSpec as P

D = 8192
HD = 128
TOK = 512
BLOCKS = 16
ROOM = 50 << 20
ALL = ("z", "x", "y", "c")
SEQ = ("z", "x")
EXP = ("y", "c")
NEG = -1e30
SCALE = math.log2(math.e) / math.sqrt(HD)

IDS = np.arange(128).reshape(4, 4, 4, 2)


def _groups(first):
    rows = []
    for y in range(4):
        for k in range(4):
            along_z, along_x = IDS[:, k, y, :], IDS[k, :, y, :]
            rows.append([int(i) for i in (along_z if first else along_x)[:, 0]])
            rows.append([int(i) for i in (along_x if first else along_z)[:, 1]])
    return rows


def _group16():
    rows = []
    for y in range(4):
        rows.append([int(i) for i in IDS[:, :, y, 0].reshape(-1)])
        rows.append([int(i) for i in IDS[:, :, y, 1].T.reshape(-1)])
    return rows


GROUP_A = _groups(True)
GROUP_B = _groups(False)
GROUP_AB = _group16()


def exchange(array, groups):
    return lax.all_to_all(array, ALL, 0, 0, tiled=True, axis_index_groups=groups)


def spread(array, groups):
    return exchange(jnp.broadcast_to(array[None], (4, *array.shape)), groups)


def pack_heads_kernel(q, k, v, o):
    for h in range(4):
        for i, ref in enumerate((q, k, v)):
            o[h, i] = ref[:, h * HD : (h + 1) * HD]


def pack_heads(queries, keys, values):
    return pl.pallas_call(
        pack_heads_kernel,
        out_shape=jax.ShapeDtypeStruct((4, 3, TOK, HD), jnp.bfloat16),
        compiler_params=pltpu.CompilerParams(vmem_limit_bytes=ROOM),
        name="pack_heads",
    )(queries, keys, values)


def pack_parts_kernel(got, q, one, two):
    for i in range(2):
        one[0, i, 0:TOK] = got[i, 1]
        one[0, i, TOK : 2 * TOK] = got[i, 2]
        one[0, i, 2 * TOK : 2 * TOK + 128] = q[i, 0]
        one[0, i, 2 * TOK + 128 :] = q[i + 2, 0]
        two[0, i, 0:TOK] = got[i + 2, 1]
        two[0, i, TOK:] = got[i + 2, 2]


def pack_parts(got):
    return pl.pallas_call(
        pack_parts_kernel,
        grid=(4,),
        in_specs=[
            pl.BlockSpec((4, 3, TOK, HD), lambda p: (0, 0, 0, 0)),
            pl.BlockSpec((4, 1, 128, HD), lambda p: (0, 0, p, 0)),
        ],
        out_specs=[
            pl.BlockSpec((1, 2, 1280, HD), lambda p: (p, 0, 0, 0)),
            pl.BlockSpec((1, 2, 1024, HD), lambda p: (p, 0, 0, 0)),
        ],
        out_shape=[
            jax.ShapeDtypeStruct((4, 2, 1280, HD), jnp.bfloat16),
            jax.ShapeDtypeStruct((4, 2, 1024, HD), jnp.bfloat16),
        ],
        compiler_params=pltpu.CompilerParams(vmem_limit_bytes=20 << 20),
        name="pack_parts",
    )(got, got)


QW = 512
TILE = QW // 128
TILES = BLOCKS // TILE


def attend_kernel(tab, r, *refs, part):
    if part == 0:
        mo, lo_, acco, qto, vt, s0, s1, sums, m, l, sem = refs
        moves = [
            pltpu.make_async_copy(sums.at[n], acco.at[n], sem.at[n]) for n in range(TILES)
        ]
    else:
        mi, li, acci, qti, o, vt, s0, s1, sums, m, l, sem = refs
        moves = [
            pltpu.make_async_copy(acci.at[n], sums.at[n], sem.at[n]) for n in range(TILES)
        ]
        for move in moves:
            move.start()
    bound, sub, core = tab[48], tab[49], tab[50]
    start = jnp.where(core == 0, 4 * part, part)

    def turn(t, carry):
        vt[t] = r[t, TOK : 2 * TOK, :].T
        return carry

    lax.fori_loop(0, 8, turn, 0)
    col = lax.broadcasted_iota(jnp.int32, (1, QW), 1)
    row = lax.broadcasted_iota(jnp.int32, (TOK, 1), 0)

    def tile(index):
        j = TILE * index
        acc = sums.at[index]
        if part == 0:
            qt = qto.at[index]
            for i in range(TILE):
                here = r[tab[j + i], pl.ds(2 * TOK + 128 * tab[32 + j + i], 128), :]
                qt[:, i * 128 : (i + 1) * 128] = here.T
            m[...] = jnp.full((1, QW), NEG, jnp.float32)
            l[...] = jnp.zeros((1, QW), jnp.float32)
            acc[...] = jnp.zeros((HD, QW), jnp.float32)
        else:
            qt = qti.at[index]
            m[...] = mi[index]
            l[...] = li[index]
            moves[index].wait()
        first = j * TOK + sub * 128
        last = first + (TILE - 1) * TOK + 127
        qpos = first + (col // 128) * TOK + col % 128
        qlow = jnp.where(qpos >= bound, bound, 0)
        lo = jnp.where(first >= bound, bound // (2 * TOK), 0)
        hi = (j + TILE) // 2
        lo = (jnp.maximum(lo - start, 0) + core) >> core
        hi = jnp.minimum((jnp.maximum(hi - start, 0) + core) >> core, 4)

        def score(t, c0=0):
            return jnp.dot(
                r[tab[t], 0:TOK, :], qt[:, c0:], preferred_element_type=jnp.float32
            )

        def soft(s, t, masked, c0=0):
            here = s[:, c0:]
            if masked:
                kpos = t * TOK + row
                here = jnp.where((kpos <= qpos[:, c0:]) & (kpos >= qlow[:, c0:]), here, NEG)
            old = m[:, c0:]
            new = jnp.maximum(old, jnp.max(here, axis=0, keepdims=True))
            p = jnp.exp2(here * SCALE - new * SCALE)
            f = jnp.exp2((old - new) * SCALE)
            m[:, c0:] = new
            l[:, c0:] = l[:, c0:] * f + jnp.sum(p, axis=0, keepdims=True)
            acc[:, c0:] = acc[:, c0:] * f + jnp.dot(
                vt[tab[t]], p.astype(jnp.bfloat16), preferred_element_type=jnp.float32
            )

        def first_of(i):
            return 2 * (start + (i << core))

        s0[...] = score(first_of(jnp.minimum(lo, 3)))

        def step(i, inner):
            t = first_of(i)

            def go(masked):
                s1[...] = score(t + 1)
                soft(s0, t, masked)
                s0[...] = score(first_of(jnp.minimum(i + 1, 3)))
                soft(s1, t + 1, masked)

            def go_half():
                half = QW // 2
                s1[:, half:] = score(t + 1, half)
                soft(s0, t, True, half)
                soft(s1, t + 1, True, half)

            need = ((t + 2) * TOK - 1 > first) | ((t * TOK < bound) & (last >= bound))
            final = t == j + 2
            pl.when(final)(go_half)
            pl.when(need & jnp.logical_not(final))(lambda: go(True))
            pl.when(jnp.logical_not(need | final))(lambda: go(False))
            return inner

        lax.fori_loop(lo, hi, step, 0)
        if part == 0:
            mo[index] = m[...]
            lo_[index] = l[...]
            moves[index].start()
        else:
            out = (acc[...] / l[...]).T.astype(jnp.bfloat16)
            for i in range(TILE):
                o[tab[16 + j + i]] = out[i * 128 : (i + 1) * 128]

    for n in range(TILES):
        tile(n)
    if part == 0:
        for move in moves:
            move.wait()


def attend(part, tab, received, *state):
    vmem = pl.BlockSpec(memory_space=pltpu.VMEM)
    anywhere = pl.BlockSpec(memory_space=pl.ANY)
    state_specs = [vmem, vmem, anywhere, vmem]
    if part == 0:
        out_shape = [
            jax.ShapeDtypeStruct((TILES, 1, QW), jnp.float32),
            jax.ShapeDtypeStruct((TILES, 1, QW), jnp.float32),
            jax.ShapeDtypeStruct((TILES, HD, QW), jnp.float32),
            jax.ShapeDtypeStruct((TILES, HD, QW), jnp.bfloat16),
        ]
    else:
        out_shape = jax.ShapeDtypeStruct((BLOCKS, 128, HD), jnp.bfloat16)
    return pl.pallas_call(
        functools.partial(attend_kernel, part=part),
        out_shape=out_shape,
        in_specs=[pl.BlockSpec(memory_space=pltpu.SMEM), vmem] + state_specs[: len(state)],
        out_specs=state_specs if part == 0 else vmem,
        scratch_shapes=[
            pltpu.VMEM((8, HD, TOK), jnp.bfloat16),
            pltpu.VMEM((TOK, QW), jnp.float32),
            pltpu.VMEM((TOK, QW), jnp.float32),
            pltpu.VMEM((TILES, HD, QW), jnp.float32),
            pltpu.VMEM((1, QW), jnp.float32),
            pltpu.VMEM((1, QW), jnp.float32),
            pltpu.SemaphoreType.DMA((TILES,)),
        ],
        compiler_params=pltpu.CompilerParams(vmem_limit_bytes=24 << 20),
        cost_estimate=pl.CostEstimate(
            flops=6_000_000_000, bytes_accessed=4_000_000, transcendentals=4_000_000
        ),
        name="attend",
    )(tab, received, *state)


def project_kernel(order, mine, theirs, w, base, o, ws, acc, sem):
    copies = []
    for k in range(8):
        rows = pl.ds(pl.multiple_of(order[k] * 512, 512), 512)
        copies.append(pltpu.make_async_copy(w.at[rows], ws.at[k], sem.at[k]))
        copies[-1].start()
    for k in range(8):
        part = (mine if k < 4 else theirs)[k % 4, 0 : acc.shape[0]]
        copies[k].wait()
        term = jnp.dot(part, ws[k], preferred_element_type=jnp.float32)
        if k == 0:
            acc[...] = base[...].astype(jnp.float32) + term
        elif k < 7:
            acc[...] += term
        else:
            total = (acc[...] + term).astype(jnp.bfloat16)
            o[...] = total.reshape(o.shape)


def project(order, mine, theirs, w, base, shape):
    rows = base.shape[0]
    vmem = pl.BlockSpec(memory_space=pltpu.VMEM)
    hbm = pl.BlockSpec(memory_space=pltpu.HBM)
    return pl.pallas_call(
        project_kernel,
        in_specs=[pl.BlockSpec(memory_space=pltpu.SMEM), vmem, vmem, hbm, vmem],
        out_specs=vmem,
        out_shape=jax.ShapeDtypeStruct(shape, jnp.bfloat16),
        scratch_shapes=[
            pltpu.VMEM((8, 512, 1024), jnp.bfloat16),
            pltpu.VMEM((rows, 1024), jnp.float32),
            pltpu.SemaphoreType.DMA((8,)),
        ],
        compiler_params=pltpu.CompilerParams(vmem_limit_bytes=ROOM),
        cost_estimate=pl.CostEstimate(
            flops=rows * 8_388_608, bytes_accessed=8_388_608 + rows * 12_288, transcendentals=0
        ),
        name="project",
    )(order, mine, theirs, w, base)


def experts_kernel(piece, gate, up, down, o, gs, us, ds, sem):
    wide = D // 4
    copies = []
    for k in range(4):
        span = pl.ds(k * wide, wide)
        copies.append(
            (
                pltpu.make_async_copy(gate.at[0, span], gs.at[k], sem.at[0, k]),
                pltpu.make_async_copy(up.at[0, span], us.at[k], sem.at[1, k]),
            )
        )
    last = [
        pltpu.make_async_copy(down.at[0, :, pl.ds(k * wide, wide)], ds.at[k], sem.at[2, k])
        for k in range(4)
    ]
    for group in (*copies, last):
        for copy in group:
            copy.start()
    g = u = None
    for k in range(4):
        for copy in copies[k]:
            copy.wait()
        rows = piece[:, k * wide : (k + 1) * wide]
        add_g = jnp.dot(rows, gs[k], preferred_element_type=jnp.float32)
        add_u = jnp.dot(rows, us[k], preferred_element_type=jnp.float32)
        g, u = (add_g, add_u) if k == 0 else (g + add_g, u + add_u)
    inner = (jax.nn.silu(g) * u).astype(jnp.bfloat16)
    for k in range(4):
        last[k].wait()
        o[:, k * wide : (k + 1) * wide] = jnp.dot(
            inner, ds[k], preferred_element_type=jnp.float32
        ).astype(o.dtype)


def experts(piece, w_gate, w_up, w_down):
    hbm = pl.BlockSpec(memory_space=pltpu.HBM)
    return pl.pallas_call(
        experts_kernel,
        in_specs=[pl.BlockSpec(memory_space=pltpu.VMEM)] + [hbm] * 3,
        out_specs=pl.BlockSpec(memory_space=pltpu.VMEM),
        out_shape=jax.ShapeDtypeStruct((128, D), jnp.bfloat16),
        scratch_shapes=[
            pltpu.VMEM((4, D // 4, 256), jnp.bfloat16),
            pltpu.VMEM((4, D // 4, 256), jnp.bfloat16),
            pltpu.VMEM((4, 256, D // 4), jnp.bfloat16),
            pltpu.SemaphoreType.DMA((3, 4)),
        ],
        compiler_params=pltpu.CompilerParams(vmem_limit_bytes=46 << 20),
        cost_estimate=pl.CostEstimate(
            flops=1_610_000_000, bytes_accessed=16_800_000, transcendentals=32_768
        ),
        name="experts",
    )(piece, w_gate, w_up, w_down)


def add_kernel(parts, o):
    total = parts[0].astype(jnp.float32)
    for n in range(1, 4):
        total += parts[n].astype(jnp.float32)
    o[...] = total.astype(o.dtype)


def add(parts):
    rows, width = parts.shape[1] // 4, parts.shape[2]
    return pl.pallas_call(
        add_kernel,
        grid=(4,),
        in_specs=[pl.BlockSpec((4, rows, width), lambda k: (0, k, 0))],
        out_specs=pl.BlockSpec((rows, width), lambda k: (k, 0)),
        out_shape=jax.ShapeDtypeStruct(parts.shape[1:], jnp.bfloat16),
        compiler_params=pltpu.CompilerParams(vmem_limit_bytes=8 << 20),
        name="add",
    )(parts)


def swap(array):
    return lax.ppermute(array, "c", [(0, 1), (1, 0)])


def ring(array, step):
    return lax.ppermute(array, "y", [(i, (i + step) % 4) for i in range(4)])


def in_three(array):
    parts = []
    for _ in range(3):
        part = lax.reduce_precision(array, 8, 7)
        parts.append(part.astype(jnp.bfloat16))
        array = array - part
    return parts


def shards(
    residual,
    queries,
    keys,
    values,
    documents,
    out_proj,
    modality,
    norm_gain,
    picks,
    router,
    w_gate,
    w_up,
    w_down,
):
    z, x, y, c = (lax.axis_index(name) for name in ALL)
    seq = z * 4 + x
    expert = y * 2 + c
    b = jnp.where(c == 0, x, z)

    got = exchange(pack_heads(queries, keys, values), GROUP_A)
    one, two = pack_parts(got)
    one = exchange(one, GROUP_B).reshape(8, 1280, HD)
    one, two = lax.optimization_barrier((one, two))
    two = exchange(two, GROUP_B).reshape(8, 1024, HD)

    index = jnp.arange(BLOCKS, dtype=jnp.int32)
    low, high = index % 4, index // 4
    from_a = jnp.where(c == 0, high, low)
    from_b = jnp.where(c == 0, low, high)
    bound = documents.shape[0] - jnp.sum(documents)
    tab = jnp.concatenate(
        [
            from_b * 2 + from_a % 2,
            from_a * 4 + from_b,
            from_a // 2,
            jnp.stack([bound, b, c]).astype(jnp.int32),
        ]
    ).astype(jnp.int32)
    ranked = picks.reshape(8, 8, 16)
    inside = (ranked // TOK) == seq
    local = jnp.sum(jnp.where(inside, ranked - seq * TOK, 0), axis=1).T.reshape(128, 1)
    filled = jnp.any(inside, axis=1).T.reshape(128, 1)
    hot = ((jnp.arange(TOK, dtype=jnp.int32)[None, :] == local) & filled).astype(jnp.bfloat16)

    base = jnp.dot(hot, residual, preferred_element_type=jnp.float32).astype(jnp.bfloat16)
    gain_sent = jnp.stack(in_three(norm_gain), axis=1).reshape(12, 512)
    gain_sent = jnp.pad(gain_sent, ((0, 4), (0, 0)))

    state = attend(0, tab, one)
    attended = attend(1, tab, two, *state)
    attended = exchange(attended, GROUP_AB)
    attended, hot, base, gain_sent = lax.optimization_barrier((attended, hot, base, gain_sent))
    attended = attended.reshape(4, TOK, HD).transpose(1, 0, 2).reshape(TOK, 4 * HD)

    early = jnp.dot(hot, attended, preferred_element_type=jnp.float32).astype(jnp.bfloat16)
    early = jnp.concatenate([early, gain_sent], axis=0)
    mine = lax.all_to_all(jnp.broadcast_to(early[None], (4, 144, 512)), "y", 0, 0, tiled=True)
    theirs = swap(mine)
    chip = jnp.arange(4, dtype=jnp.int32)
    order = jnp.concatenate([2 * chip + c, 2 * chip + 1 - c]).astype(jnp.int32)
    rows = project(order, mine, theirs, out_proj, base, (128, 8, 128))
    gains = jnp.stack([mine[:, 128:140], theirs[:, 128:140]]).reshape(2, 4, 2, 3, 1024)
    gains = jnp.where(expert < 4, gains[:, :, 0], gains[:, :, 1]).astype(jnp.float32)
    gains = gains[:, :, 0] + (gains[:, :, 1] + gains[:, :, 2])
    gains = jnp.where(c == 0, gains, gains[::-1])
    gain = gains.transpose(1, 0, 2).reshape(1, D)

    held, rows = lax.optimization_barrier((attended, rows))
    arrived = lax.all_to_all(rows, ALL, 0, 0, tiled=True)
    before = ring(held, 1)
    after = ring(held, -1)
    half = TOK // 2
    opposite = jnp.concatenate([ring(before[:half], 1), ring(after[half:], -1)], axis=0)
    mine = jnp.stack([held, before, after, opposite])
    theirs = swap(mine)
    chip = jnp.remainder(y + jnp.array([0, 3, 1, 2], jnp.int32), 4)
    order = jnp.concatenate([2 * chip + c, 2 * chip + 1 - c]).astype(jnp.int32)
    own = lax.dynamic_index_in_dim(ranked, expert, 0, keepdims=False)
    own = lax.dynamic_index_in_dim(own, seq, 1, keepdims=False)
    source = (own // TOK)[:, None] == jnp.arange(16, dtype=jnp.int32)[None, :]
    source = source.astype(jnp.bfloat16)
    taken = jnp.dot(source, arrived.reshape(16, D), preferred_element_type=jnp.float32)
    inverse = lax.rsqrt(jnp.mean(taken * taken, axis=1, keepdims=True) + 1e-05)
    chosen = (taken * inverse * gain).astype(jnp.bfloat16)
    logits = jnp.dot(chosen, router, preferred_element_type=jnp.float32)
    near = spread(chosen, GROUP_A)
    far = spread(near.reshape(32, D), GROUP_B)
    piece = far.reshape(128, D)
    partial = experts(piece, w_gate, w_up, w_down)
    partial = exchange(partial.reshape(4, 32, D), GROUP_B)
    partial = add(partial)
    partial = exchange(partial.reshape(4, 8, D), GROUP_A)
    summed = jnp.sum(partial.astype(jnp.float32), axis=0)
    weighted = (jax.nn.sigmoid(logits) * summed).astype(jnp.bfloat16)
    back = lax.dot_general(
        source, weighted, (((0,), (0,)), ((), ())), preferred_element_type=jnp.float32
    ).astype(jnp.bfloat16)
    back, mine, theirs = lax.optimization_barrier((back, mine, theirs))
    hidden = project(order, mine, theirs, out_proj, residual, (TOK, 1024))
    returned = lax.all_to_all(back.reshape(128, 8, 128), ALL, 0, 0, tiled=True)
    expert_add = lax.dot_general(
        hot, returned.reshape(128, 1024), (((0,), (0,)), ((), ())), preferred_element_type=jnp.float32
    )
    return (hidden.astype(jnp.float32) + expert_add).astype(jnp.bfloat16)


def solution(mesh):
    finer = Mesh(mesh.devices.reshape(4, 4, 4, 2), ALL)
    in_specs = (
        P(SEQ, EXP),
        P(SEQ, EXP),
        P(SEQ, EXP),
        P(SEQ, EXP),
        P(),
        P(None, EXP),
        P(SEQ),
        P(None, EXP),
        P(),
        P(None, EXP),
        P(EXP, None, SEQ),
        P(EXP, None, SEQ),
        P(EXP, SEQ, None),
    )
    return jax.shard_map(
        shards, mesh=finer, in_specs=in_specs, out_specs=P(SEQ, EXP), check_vma=False
    )
```

```python
import functools
import math

import jax
import jax.numpy as jnp
import numpy as np
from jax import lax
from jax.experimental import pallas as pl
from jax.experimental.pallas import tpu as pltpu
from jax.sharding import Mesh
from jax.sharding import PartitionSpec as P

D = 8192
HD = 128
TOK = 512
BLOCKS = 16
ALL = ("z", "x", "y", "c")
SEQ = ("z", "x")
EXP = ("y", "c")
NEG = -1e30
SCALE = math.log2(math.e) / math.sqrt(HD)

IDS = np.arange(128).reshape(4, 4, 4, 2)


def _groups(first):
    rows = []
    for y in range(4):
        for k in range(4):
            along_z, along_x = IDS[:, k, y, :], IDS[k, :, y, :]
            rows.append([int(i) for i in (along_z if first else along_x)[:, 0]])
            rows.append([int(i) for i in (along_x if first else along_z)[:, 1]])
    return rows


def _group16():
    rows = []
    for y in range(4):
        rows.append([int(i) for i in IDS[:, :, y, 0].reshape(-1)])
        rows.append([int(i) for i in IDS[:, :, y, 1].T.reshape(-1)])
    return rows


GROUP_A = _groups(True)
GROUP_B = _groups(False)
GROUP_AB = _group16()


def exchange(array, groups):
    return lax.all_to_all(array, ALL, 0, 0, tiled=True, axis_index_groups=groups)


def spread(array, groups):
    return exchange(jnp.broadcast_to(array[None], (4, *array.shape)), groups)


def in_hbm(array):
    return pltpu.with_memory_space_constraint(array, pltpu.HBM)


def pack_heads_kernel(q, k, v, o, held, sem):
    reads = []
    for h in range(4):
        for i, ref in enumerate((q, k, v)):
            part = ref.at[:, pl.ds(h * HD, HD)]
            reads.append(pltpu.make_async_copy(part, held.at[h, i], sem.at[0, h, i]))
            reads[-1].start()
    writes = []
    for n, read in enumerate(reads):
        read.wait()
        h, i = n // 3, n % 3
        writes.append(pltpu.make_async_copy(held.at[h, i], o.at[h, i], sem.at[1, h, i]))
        writes[-1].start()
    for write in writes:
        write.wait()


def pack_heads(queries, keys, values):
    hbm = pl.BlockSpec(memory_space=pltpu.HBM)
    return pl.pallas_call(
        pack_heads_kernel,
        in_specs=[hbm] * 3,
        out_specs=hbm,
        out_shape=pltpu.HBM((4, 3, TOK, HD), jnp.bfloat16),
        scratch_shapes=[
            pltpu.VMEM((4, 3, TOK, HD), jnp.bfloat16),
            pltpu.SemaphoreType.DMA((2, 4, 3)),
        ],
        name="pack_heads",
    )(in_hbm(queries), in_hbm(keys), in_hbm(values))


def pack_parts_kernel(got, q, one, two):
    for i in range(2):
        one[0, i, 0:TOK] = got[i, 1]
        one[0, i, TOK : 2 * TOK] = got[i, 2]
        one[0, i, 2 * TOK : 2 * TOK + 128] = q[i, 0]
        one[0, i, 2 * TOK + 128 :] = q[i + 2, 0]
        two[0, i, 0:TOK] = got[i + 2, 1]
        two[0, i, TOK:] = got[i + 2, 2]


def pack_parts(got):
    return pl.pallas_call(
        pack_parts_kernel,
        grid=(4,),
        in_specs=[
            pl.BlockSpec((4, 3, TOK, HD), lambda p: (0, 0, 0, 0)),
            pl.BlockSpec((4, 1, 128, HD), lambda p: (0, 0, p, 0)),
        ],
        out_specs=[
            pl.BlockSpec((1, 2, 1280, HD), lambda p: (p, 0, 0, 0)),
            pl.BlockSpec((1, 2, 1024, HD), lambda p: (p, 0, 0, 0)),
        ],
        out_shape=[
            jax.ShapeDtypeStruct((4, 2, 1280, HD), jnp.bfloat16),
            jax.ShapeDtypeStruct((4, 2, 1024, HD), jnp.bfloat16),
        ],
        compiler_params=pltpu.CompilerParams(vmem_limit_bytes=20 << 20),
        name="pack_parts",
    )(got, got)


QW = 512
TILE = QW // 128
TILES = BLOCKS // TILE


def attend_kernel(tab, r, *refs, part):
    if part == 0:
        mo, lo_, acco, qto, vt, s0, s1, sums, turned, m, l, sem = refs
        moves = [
            (
                pltpu.make_async_copy(turned.at[n], qto.at[n], sem.at[0, n]),
                pltpu.make_async_copy(sums.at[n], acco.at[n], sem.at[1, n]),
            )
            for n in range(TILES)
        ]
    else:
        mi, li, acci, qti, o, vt, s0, s1, sums, turned, m, l, sem = refs
        moves = [
            (
                pltpu.make_async_copy(qti.at[n], turned.at[n], sem.at[0, n]),
                pltpu.make_async_copy(acci.at[n], sums.at[n], sem.at[1, n]),
            )
            for n in range(TILES)
        ]
        for move in moves:
            move[0].start()
            move[1].start()
    bound, sub, core = tab[48], tab[49], tab[50]
    start = jnp.where(core == 0, 4 * part, part)

    def turn(t, carry):
        vt[t] = r[t, TOK : 2 * TOK, :].T
        return carry

    lax.fori_loop(0, 8, turn, 0)
    col = lax.broadcasted_iota(jnp.int32, (1, QW), 1)
    row = lax.broadcasted_iota(jnp.int32, (TOK, 1), 0)

    def tile(index):
        j = TILE * index
        acc = sums.at[index]
        qt = turned.at[index]
        if part == 0:
            for i in range(TILE):
                here = r[tab[j + i], pl.ds(2 * TOK + 128 * tab[32 + j + i], 128), :]
                qt[:, i * 128 : (i + 1) * 128] = here.T
            m[...] = jnp.full((1, QW), NEG, jnp.float32)
            l[...] = jnp.zeros((1, QW), jnp.float32)
            acc[...] = jnp.zeros((HD, QW), jnp.float32)
        else:
            m[...] = mi[index]
            l[...] = li[index]
            moves[index][0].wait()
            moves[index][1].wait()
        first = j * TOK + sub * 128
        last = first + (TILE - 1) * TOK + 127
        qpos = first + (col // 128) * TOK + col % 128
        qlow = jnp.where(qpos >= bound, bound, 0)
        lo = jnp.where(first >= bound, bound // (2 * TOK), 0)
        hi = (j + TILE) // 2
        lo = (jnp.maximum(lo - start, 0) + core) >> core
        hi = jnp.minimum((jnp.maximum(hi - start, 0) + core) >> core, 4)

        def score(t, c0=0):
            return jnp.dot(
                r[tab[t], 0:TOK, :], qt[:, c0:], preferred_element_type=jnp.float32
            )

        def soft(s, t, masked, c0=0):
            here = s[:, c0:]
            if masked:
                kpos = t * TOK + row
                here = jnp.where((kpos <= qpos[:, c0:]) & (kpos >= qlow[:, c0:]), here, NEG)
            old = m[:, c0:]
            new = jnp.maximum(old, jnp.max(here, axis=0, keepdims=True))
            p = jnp.exp2(here * SCALE - new * SCALE)
            f = jnp.exp2((old - new) * SCALE)
            m[:, c0:] = new
            l[:, c0:] = l[:, c0:] * f + jnp.sum(p, axis=0, keepdims=True)
            acc[:, c0:] = acc[:, c0:] * f + jnp.dot(
                vt[tab[t]], p.astype(jnp.bfloat16), preferred_element_type=jnp.float32
            )

        def first_of(i):
            return 2 * (start + (i << core))

        s0[...] = score(first_of(jnp.minimum(lo, 3)))

        def step(i, inner):
            t = first_of(i)

            def go(masked):
                s1[...] = score(t + 1)
                soft(s0, t, masked)
                s0[...] = score(first_of(jnp.minimum(i + 1, 3)))
                soft(s1, t + 1, masked)

            def go_half():
                half = QW // 2
                s1[:, half:] = score(t + 1, half)
                soft(s0, t, True, half)
                soft(s1, t + 1, True, half)

            need = ((t + 2) * TOK - 1 > first) | ((t * TOK < bound) & (last >= bound))
            final = t == j + 2
            pl.when(final)(go_half)
            pl.when(need & jnp.logical_not(final))(lambda: go(True))
            pl.when(jnp.logical_not(need | final))(lambda: go(False))
            return inner

        lax.fori_loop(lo, hi, step, 0)
        if part == 0:
            mo[index] = m[...]
            lo_[index] = l[...]
            moves[index][0].start()
            moves[index][1].start()
        else:
            out = (acc[...] / l[...]).T.astype(jnp.bfloat16)
            for i in range(TILE):
                o[tab[16 + j + i]] = out[i * 128 : (i + 1) * 128]

    for n in range(TILES):
        tile(n)
    if part == 0:
        for move in moves:
            move[0].wait()
            move[1].wait()


def attend(part, tab, received, *state):
    vmem = pl.BlockSpec(memory_space=pltpu.VMEM)
    anywhere = pl.BlockSpec(memory_space=pltpu.HBM)
    state_specs = [vmem, vmem, anywhere, anywhere]
    state = [*state[:2], *(in_hbm(a) for a in state[2:])]
    if part == 0:
        out_shape = [
            jax.ShapeDtypeStruct((TILES, 1, QW), jnp.float32),
            jax.ShapeDtypeStruct((TILES, 1, QW), jnp.float32),
            pltpu.HBM((TILES, HD, QW), jnp.float32),
            pltpu.HBM((TILES, HD, QW), jnp.bfloat16),
        ]
    else:
        out_shape = jax.ShapeDtypeStruct((BLOCKS, 128, HD), jnp.bfloat16)
    return pl.pallas_call(
        functools.partial(attend_kernel, part=part),
        out_shape=out_shape,
        in_specs=[pl.BlockSpec(memory_space=pltpu.SMEM), vmem] + state_specs[: len(state)],
        out_specs=state_specs if part == 0 else vmem,
        scratch_shapes=[
            pltpu.VMEM((8, HD, TOK), jnp.bfloat16),
            pltpu.VMEM((TOK, QW), jnp.float32),
            pltpu.VMEM((TOK, QW), jnp.float32),
            pltpu.VMEM((TILES, HD, QW), jnp.float32),
            pltpu.VMEM((TILES, HD, QW), jnp.bfloat16),
            pltpu.VMEM((1, QW), jnp.float32),
            pltpu.VMEM((1, QW), jnp.float32),
            pltpu.SemaphoreType.DMA((2, TILES)),
        ],
        compiler_params=pltpu.CompilerParams(vmem_limit_bytes=24 << 20),
        cost_estimate=pl.CostEstimate(
            flops=6_000_000_000, bytes_accessed=4_000_000, transcendentals=4_000_000
        ),
        name="attend",
    )(tab, received, *state)


def project_kernel(order, mine, theirs, w, base, o, ws, acc, sem):
    copies = []
    for k in range(8):
        rows = pl.ds(pl.multiple_of(order[k] * 512, 512), 512)
        copies.append(pltpu.make_async_copy(w.at[rows], ws.at[k], sem.at[k]))
        copies[-1].start()
    for k in range(8):
        part = (mine if k < 4 else theirs)[k % 4, 0 : acc.shape[0]]
        copies[k].wait()
        term = jnp.dot(part, ws[k], preferred_element_type=jnp.float32)
        if k == 0:
            acc[...] = base[...].astype(jnp.float32) + term
        elif k < 7:
            acc[...] += term
        else:
            total = (acc[...] + term).astype(jnp.bfloat16)
            o[...] = total.reshape(o.shape)


def project(order, mine, theirs, w, base, shape):
    rows = base.shape[0]
    vmem = pl.BlockSpec(memory_space=pltpu.VMEM)
    hbm = pl.BlockSpec(memory_space=pltpu.HBM)
    return pl.pallas_call(
        project_kernel,
        in_specs=[pl.BlockSpec(memory_space=pltpu.SMEM), vmem, vmem, hbm, vmem],
        out_specs=vmem,
        out_shape=jax.ShapeDtypeStruct(shape, jnp.bfloat16),
        scratch_shapes=[
            pltpu.VMEM((8, 512, 1024), jnp.bfloat16),
            pltpu.VMEM((rows, 1024), jnp.float32),
            pltpu.SemaphoreType.DMA((8,)),
        ],
        compiler_params=pltpu.CompilerParams(vmem_limit_bytes=24 << 20),
        cost_estimate=pl.CostEstimate(
            flops=rows * 8_388_608, bytes_accessed=8_388_608 + rows * 12_288, transcendentals=0
        ),
        name="project",
    )(order, mine, theirs, in_hbm(w), base)


def experts_kernel(piece, gate, up, down, o, gs, us, ds, out, sem):
    wide = D // 4
    copies = []
    for k in range(4):
        span = pl.ds(k * wide, wide)
        copies.append(
            (
                pltpu.make_async_copy(gate.at[0, span], gs.at[k], sem.at[0, k]),
                pltpu.make_async_copy(up.at[0, span], us.at[k], sem.at[1, k]),
            )
        )
    last = [
        pltpu.make_async_copy(down.at[0, :, pl.ds(k * wide, wide)], ds.at[k], sem.at[2, k])
        for k in range(4)
    ]
    for group in (*copies, last):
        for copy in group:
            copy.start()
    g = u = None
    for k in range(4):
        for copy in copies[k]:
            copy.wait()
        rows = piece[:, k * wide : (k + 1) * wide]
        add_g = jnp.dot(rows, gs[k], preferred_element_type=jnp.float32)
        add_u = jnp.dot(rows, us[k], preferred_element_type=jnp.float32)
        g, u = (add_g, add_u) if k == 0 else (g + add_g, u + add_u)
    inner = (jax.nn.silu(g) * u).astype(jnp.bfloat16)
    for k in range(4):
        last[k].wait()
        out[k] = jnp.dot(inner, ds[k], preferred_element_type=jnp.float32).astype(o.dtype)
        written = pltpu.make_async_copy(
            out.at[k], o.at[:, pl.ds(k * wide, wide)], sem.at[3, k]
        )
        written.start()
        last[k] = written
    for written in last:
        written.wait()


def experts(piece, w_gate, w_up, w_down):
    hbm = pl.BlockSpec(memory_space=pltpu.HBM)
    return pl.pallas_call(
        experts_kernel,
        in_specs=[pl.BlockSpec(memory_space=pltpu.VMEM)] + [hbm] * 3,
        out_specs=hbm,
        out_shape=pltpu.HBM((128, D), jnp.bfloat16),
        scratch_shapes=[
            pltpu.VMEM((4, D // 4, 256), jnp.bfloat16),
            pltpu.VMEM((4, D // 4, 256), jnp.bfloat16),
            pltpu.VMEM((4, 256, D // 4), jnp.bfloat16),
            pltpu.VMEM((4, 128, D // 4), jnp.bfloat16),
            pltpu.SemaphoreType.DMA((4, 4)),
        ],
        compiler_params=pltpu.CompilerParams(vmem_limit_bytes=24 << 20),
        cost_estimate=pl.CostEstimate(
            flops=1_610_000_000, bytes_accessed=16_800_000, transcendentals=32_768
        ),
        name="experts",
    )(piece, in_hbm(w_gate), in_hbm(w_up), in_hbm(w_down))


def add_kernel(parts, o):
    total = parts[0].astype(jnp.float32)
    for n in range(1, 4):
        total += parts[n].astype(jnp.float32)
    o[...] = total.astype(o.dtype)


def add(parts):
    rows, width = parts.shape[1] // 4, parts.shape[2]
    return pl.pallas_call(
        add_kernel,
        grid=(4,),
        in_specs=[pl.BlockSpec((4, rows, width), lambda k: (0, k, 0))],
        out_specs=pl.BlockSpec((rows, width), lambda k: (k, 0)),
        out_shape=jax.ShapeDtypeStruct(parts.shape[1:], jnp.bfloat16),
        compiler_params=pltpu.CompilerParams(vmem_limit_bytes=8 << 20),
        name="add",
    )(parts)


def swap(array):
    return lax.ppermute(array, "c", [(0, 1), (1, 0)])


def ring(array, step):
    return lax.ppermute(array, "y", [(i, (i + step) % 4) for i in range(4)])


def in_three(array):
    parts = []
    for _ in range(3):
        part = lax.reduce_precision(array, 8, 7)
        parts.append(part.astype(jnp.bfloat16))
        array = array - part
    return parts


def shards(
    residual,
    queries,
    keys,
    values,
    documents,
    out_proj,
    modality,
    norm_gain,
    picks,
    router,
    w_gate,
    w_up,
    w_down,
):
    z, x, y, c = (lax.axis_index(name) for name in ALL)
    seq = z * 4 + x
    expert = y * 2 + c
    b = jnp.where(c == 0, x, z)

    got = exchange(pack_heads(queries, keys, values), GROUP_A)
    one, two = pack_parts(got)
    one = exchange(one, GROUP_B).reshape(8, 1280, HD)
    one, two = lax.optimization_barrier((one, two))
    two = exchange(two, GROUP_B).reshape(8, 1024, HD)

    index = jnp.arange(BLOCKS, dtype=jnp.int32)
    low, high = index % 4, index // 4
    from_a = jnp.where(c == 0, high, low)
    from_b = jnp.where(c == 0, low, high)
    bound = documents.shape[0] - jnp.sum(documents)
    tab = jnp.concatenate(
        [
            from_b * 2 + from_a % 2,
            from_a * 4 + from_b,
            from_a // 2,
            jnp.stack([bound, b, c]).astype(jnp.int32),
        ]
    ).astype(jnp.int32)
    ranked = picks.reshape(8, 8, 16)
    inside = (ranked // TOK) == seq
    local = jnp.sum(jnp.where(inside, ranked - seq * TOK, 0), axis=1).T.reshape(128, 1)
    filled = jnp.any(inside, axis=1).T.reshape(128, 1)
    hot = ((jnp.arange(TOK, dtype=jnp.int32)[None, :] == local) & filled).astype(jnp.bfloat16)

    base = jnp.dot(hot, residual, preferred_element_type=jnp.float32).astype(jnp.bfloat16)
    gain_sent = jnp.stack(in_three(norm_gain), axis=1).reshape(12, 512)
    gain_sent = jnp.pad(gain_sent, ((0, 4), (0, 0)))

    state = attend(0, tab, one)
    attended = attend(1, tab, two, *state)
    attended = exchange(attended, GROUP_AB)
    attended, hot, base, gain_sent = lax.optimization_barrier((attended, hot, base, gain_sent))
    attended = attended.reshape(4, TOK, HD).transpose(1, 0, 2).reshape(TOK, 4 * HD)

    early = jnp.dot(hot, attended, preferred_element_type=jnp.float32).astype(jnp.bfloat16)
    early = jnp.concatenate([early, gain_sent], axis=0)
    mine = lax.all_to_all(jnp.broadcast_to(early[None], (4, 144, 512)), "y", 0, 0, tiled=True)
    theirs = swap(mine)
    chip = jnp.arange(4, dtype=jnp.int32)
    order = jnp.concatenate([2 * chip + c, 2 * chip + 1 - c]).astype(jnp.int32)
    rows = project(order, mine, theirs, out_proj, base, (128, 8, 128))
    gains = jnp.stack([mine[:, 128:140], theirs[:, 128:140]]).reshape(2, 4, 2, 3, 1024)
    gains = jnp.where(expert < 4, gains[:, :, 0], gains[:, :, 1]).astype(jnp.float32)
    gains = gains[:, :, 0] + (gains[:, :, 1] + gains[:, :, 2])
    gains = jnp.where(c == 0, gains, gains[::-1])
    gain = gains.transpose(1, 0, 2).reshape(1, D)

    held, rows = lax.optimization_barrier((attended, rows))
    arrived = lax.all_to_all(rows, ALL, 0, 0, tiled=True)
    before = ring(held, 1)
    after = ring(held, -1)
    half = TOK // 2
    opposite = jnp.concatenate([ring(before[:half], 1), ring(after[half:], -1)], axis=0)
    mine = jnp.stack([held, before, after, opposite])
    theirs = swap(mine)
    chip = jnp.remainder(y + jnp.array([0, 3, 1, 2], jnp.int32), 4)
    order = jnp.concatenate([2 * chip + c, 2 * chip + 1 - c]).astype(jnp.int32)
    own = lax.dynamic_index_in_dim(ranked, expert, 0, keepdims=False)
    own = lax.dynamic_index_in_dim(own, seq, 1, keepdims=False)
    source = (own // TOK)[:, None] == jnp.arange(16, dtype=jnp.int32)[None, :]
    source = source.astype(jnp.bfloat16)
    taken = jnp.dot(source, arrived.reshape(16, D), preferred_element_type=jnp.float32)
    inverse = lax.rsqrt(jnp.mean(taken * taken, axis=1, keepdims=True) + 1e-05)
    chosen = (taken * inverse * gain).astype(jnp.bfloat16)
    logits = jnp.dot(chosen, router, preferred_element_type=jnp.float32)
    near = spread(chosen, GROUP_A)
    far = spread(near.reshape(32, D), GROUP_B)
    piece = far.reshape(128, D)
    partial = experts(piece, w_gate, w_up, w_down)
    partial = exchange(partial.reshape(4, 32, D), GROUP_B)
    partial = add(partial)
    partial = exchange(partial.reshape(4, 8, D), GROUP_A)
    summed = jnp.sum(partial.astype(jnp.float32), axis=0)
    weighted = (jax.nn.sigmoid(logits) * summed).astype(jnp.bfloat16)
    back = lax.dot_general(
        source, weighted, (((0,), (0,)), ((), ())), preferred_element_type=jnp.float32
    ).astype(jnp.bfloat16)
    back, mine, theirs = lax.optimization_barrier((back, mine, theirs))
    hidden = project(order, mine, theirs, out_proj, residual, (TOK, 1024))
    returned = lax.all_to_all(back.reshape(128, 8, 128), ALL, 0, 0, tiled=True)
    expert_add = lax.dot_general(
        hot, returned.reshape(128, 1024), (((0,), (0,)), ((), ())), preferred_element_type=jnp.float32
    )
    return (hidden.astype(jnp.float32) + expert_add).astype(jnp.bfloat16)


def solution(mesh):
    finer = Mesh(mesh.devices.reshape(4, 4, 4, 2), ALL)
    in_specs = (
        P(SEQ, EXP),
        P(SEQ, EXP),
        P(SEQ, EXP),
        P(SEQ, EXP),
        P(),
        P(None, EXP),
        P(SEQ),
        P(None, EXP),
        P(),
        P(None, EXP),
        P(EXP, None, SEQ),
        P(EXP, None, SEQ),
        P(EXP, SEQ, None),
    )
    return jax.shard_map(
        shards, mesh=finer, in_specs=in_specs, out_specs=P(SEQ, EXP), check_vma=False
    )
```

```python
import functools
import math

import jax
import jax.numpy as jnp
import numpy as np
from jax import lax
from jax.experimental import pallas as pl
from jax.experimental.pallas import tpu as pltpu
from jax.sharding import Mesh
from jax.sharding import PartitionSpec as P

D = 8192
HD = 128
TOK = 512
BLOCKS = 16
ALL = ("z", "x", "y", "c")
SEQ = ("z", "x")
EXP = ("y", "c")
NEG = -1e30
SCALE = math.log2(math.e) / math.sqrt(HD)

IDS = np.arange(128).reshape(4, 4, 4, 2)


def _groups(first):
    rows = []
    for y in range(4):
        for k in range(4):
            along_z, along_x = IDS[:, k, y, :], IDS[k, :, y, :]
            rows.append([int(i) for i in (along_z if first else along_x)[:, 0]])
            rows.append([int(i) for i in (along_x if first else along_z)[:, 1]])
    return rows


def _group16():
    rows = []
    for y in range(4):
        rows.append([int(i) for i in IDS[:, :, y, 0].reshape(-1)])
        rows.append([int(i) for i in IDS[:, :, y, 1].T.reshape(-1)])
    return rows


GROUP_A = _groups(True)
GROUP_B = _groups(False)
GROUP_AB = _group16()


def exchange(array, groups):
    return lax.all_to_all(array, ALL, 0, 0, tiled=True, axis_index_groups=groups)


def spread(array, groups):
    return exchange(jnp.broadcast_to(array[None], (4, *array.shape)), groups)


def in_hbm(array):
    return pltpu.with_memory_space_constraint(array, pltpu.HBM)


def pack_heads_kernel(q, k, v, o, held, sem):
    reads = []
    for h in range(4):
        for i, ref in enumerate((q, k, v)):
            part = ref.at[:, pl.ds(h * HD, HD)]
            reads.append(pltpu.make_async_copy(part, held.at[h, i], sem.at[0, h, i]))
            reads[-1].start()
    writes = []
    for n, read in enumerate(reads):
        read.wait()
        h, i = n // 3, n % 3
        writes.append(pltpu.make_async_copy(held.at[h, i], o.at[h, i], sem.at[1, h, i]))
        writes[-1].start()
    for write in writes:
        write.wait()


def pack_heads(queries, keys, values):
    hbm = pl.BlockSpec(memory_space=pltpu.HBM)
    return pl.pallas_call(
        pack_heads_kernel,
        in_specs=[hbm] * 3,
        out_specs=hbm,
        out_shape=pltpu.HBM((4, 3, TOK, HD), jnp.bfloat16),
        scratch_shapes=[
            pltpu.VMEM((4, 3, TOK, HD), jnp.bfloat16),
            pltpu.SemaphoreType.DMA((2, 4, 3)),
        ],
        name="pack_heads",
    )(in_hbm(queries), in_hbm(keys), in_hbm(values))


def pack_parts_kernel(got, q, one, two):
    for i in range(2):
        one[0, i, 0:TOK] = got[i, 1]
        one[0, i, TOK : 2 * TOK] = got[i, 2]
        one[0, i, 2 * TOK : 2 * TOK + 128] = q[i, 0]
        one[0, i, 2 * TOK + 128 :] = q[i + 2, 0]
        two[0, i, 0:TOK] = got[i + 2, 1]
        two[0, i, TOK:] = got[i + 2, 2]


def pack_parts(got):
    return pl.pallas_call(
        pack_parts_kernel,
        grid=(4,),
        in_specs=[
            pl.BlockSpec((4, 3, TOK, HD), lambda p: (0, 0, 0, 0)),
            pl.BlockSpec((4, 1, 128, HD), lambda p: (0, 0, p, 0)),
        ],
        out_specs=[
            pl.BlockSpec((1, 2, 1280, HD), lambda p: (p, 0, 0, 0)),
            pl.BlockSpec((1, 2, 1024, HD), lambda p: (p, 0, 0, 0)),
        ],
        out_shape=[
            jax.ShapeDtypeStruct((4, 2, 1280, HD), jnp.bfloat16),
            jax.ShapeDtypeStruct((4, 2, 1024, HD), jnp.bfloat16),
        ],
        compiler_params=pltpu.CompilerParams(vmem_limit_bytes=20 << 20),
        name="pack_parts",
    )(got, got)


QW = 512
TILE = QW // 128
TILES = BLOCKS // TILE


def attend_kernel(tab, r, *refs, part):
    if part == 0:
        mo, lo_, acco, qto, vt, s0, s1, sums, turned, m, l, sem = refs
        moves = [
            (
                pltpu.make_async_copy(turned.at[n], qto.at[n], sem.at[0, n]),
                pltpu.make_async_copy(sums.at[n], acco.at[n], sem.at[1, n]),
            )
            for n in range(TILES)
        ]
    else:
        mi, li, acci, qti, o, vt, s0, s1, sums, turned, m, l, sem, held, got = refs
        parts = [pltpu.make_async_copy(r.at[n], held.at[n], got.at[n]) for n in range(8)]
        for part_copy in parts:
            part_copy.start()
        r = held
        moves = [
            (
                pltpu.make_async_copy(qti.at[n], turned.at[n], sem.at[0, n]),
                pltpu.make_async_copy(acci.at[n], sums.at[n], sem.at[1, n]),
            )
            for n in range(TILES)
        ]
        for move in moves:
            move[0].start()
            move[1].start()
    bound, sub, core = tab[48], tab[49], tab[50]
    start = jnp.where(core == 0, 4 * part, part)

    for t in range(8):
        if part == 1:
            parts[t].wait()
        vt[t] = r[t, TOK : 2 * TOK, :].T
    col = lax.broadcasted_iota(jnp.int32, (1, QW), 1)
    row = lax.broadcasted_iota(jnp.int32, (TOK, 1), 0)

    def tile(index):
        j = TILE * index
        acc = sums.at[index]
        qt = turned.at[index]
        if part == 0:
            for i in range(TILE):
                here = r[tab[j + i], pl.ds(2 * TOK + 128 * tab[32 + j + i], 128), :]
                qt[:, i * 128 : (i + 1) * 128] = here.T
            m[...] = jnp.full((1, QW), NEG, jnp.float32)
            l[...] = jnp.zeros((1, QW), jnp.float32)
            acc[...] = jnp.zeros((HD, QW), jnp.float32)
        else:
            m[...] = mi[index]
            l[...] = li[index]
            moves[index][0].wait()
            moves[index][1].wait()
        first = j * TOK + sub * 128
        last = first + (TILE - 1) * TOK + 127
        qpos = first + (col // 128) * TOK + col % 128
        qlow = jnp.where(qpos >= bound, bound, 0)
        lo = jnp.where(first >= bound, bound // (2 * TOK), 0)
        hi = (j + TILE) // 2
        lo = (jnp.maximum(lo - start, 0) + core) >> core
        hi = jnp.minimum((jnp.maximum(hi - start, 0) + core) >> core, 4)

        def score(t, c0=0):
            return jnp.dot(
                r[tab[t], 0:TOK, :], qt[:, c0:], preferred_element_type=jnp.float32
            )

        def soft(s, t, masked, c0=0):
            here = s[:, c0:]
            if masked:
                kpos = t * TOK + row
                here = jnp.where((kpos <= qpos[:, c0:]) & (kpos >= qlow[:, c0:]), here, NEG)
            old = m[:, c0:]
            new = jnp.maximum(old, jnp.max(here, axis=0, keepdims=True))
            p = jnp.exp2(here * SCALE - new * SCALE)
            f = jnp.exp2((old - new) * SCALE)
            m[:, c0:] = new
            l[:, c0:] = l[:, c0:] * f + jnp.sum(p, axis=0, keepdims=True)
            acc[:, c0:] = acc[:, c0:] * f + jnp.dot(
                vt[tab[t]], p.astype(jnp.bfloat16), preferred_element_type=jnp.float32
            )

        def first_of(i):
            return 2 * (start + (i << core))

        s0[...] = score(first_of(jnp.minimum(lo, 3)))

        def step(i, inner):
            t = first_of(i)

            def go(masked):
                s1[...] = score(t + 1)
                soft(s0, t, masked)
                s0[...] = score(first_of(jnp.minimum(i + 1, 3)))
                soft(s1, t + 1, masked)

            def go_half():
                half = QW // 2
                s1[:, half:] = score(t + 1, half)
                soft(s0, t, True, half)
                soft(s1, t + 1, True, half)

            need = ((t + 2) * TOK - 1 > first) | ((t * TOK < bound) & (last >= bound))
            final = t == j + 2
            pl.when(final)(go_half)
            pl.when(need & jnp.logical_not(final))(lambda: go(True))
            pl.when(jnp.logical_not(need | final))(lambda: go(False))
            return inner

        lax.fori_loop(lo, hi, step, 0)
        if part == 0:
            mo[index] = m[...]
            lo_[index] = l[...]
            moves[index][0].start()
            moves[index][1].start()
        else:
            out = (acc[...] / l[...]).T.astype(jnp.bfloat16)
            for i in range(TILE):
                o[tab[16 + j + i]] = out[i * 128 : (i + 1) * 128]

    for n in range(TILES):
        tile(n)
    if part == 0:
        for move in moves:
            move[0].wait()
            move[1].wait()


def attend(part, tab, received, *state):
    vmem = pl.BlockSpec(memory_space=pltpu.VMEM)
    anywhere = pl.BlockSpec(memory_space=pltpu.HBM)
    state_specs = [vmem, vmem, anywhere, anywhere]
    state = [*state[:2], *(in_hbm(a) for a in state[2:])]
    if part == 0:
        out_shape = [
            jax.ShapeDtypeStruct((TILES, 1, QW), jnp.float32),
            jax.ShapeDtypeStruct((TILES, 1, QW), jnp.float32),
            pltpu.HBM((TILES, HD, QW), jnp.float32),
            pltpu.HBM((TILES, HD, QW), jnp.bfloat16),
        ]
    else:
        out_shape = jax.ShapeDtypeStruct((BLOCKS, 128, HD), jnp.bfloat16)
    second = [pltpu.VMEM((8, 1024, HD), jnp.bfloat16), pltpu.SemaphoreType.DMA((8,))] * part
    return pl.pallas_call(
        functools.partial(attend_kernel, part=part),
        out_shape=out_shape,
        in_specs=[pl.BlockSpec(memory_space=pltpu.SMEM), anywhere if part else vmem]
        + state_specs[: len(state)],
        out_specs=state_specs if part == 0 else vmem,
        scratch_shapes=[
            pltpu.VMEM((8, HD, TOK), jnp.bfloat16),
            pltpu.VMEM((TOK, QW), jnp.float32),
            pltpu.VMEM((TOK, QW), jnp.float32),
            pltpu.VMEM((TILES, HD, QW), jnp.float32),
            pltpu.VMEM((TILES, HD, QW), jnp.bfloat16),
            pltpu.VMEM((1, QW), jnp.float32),
            pltpu.VMEM((1, QW), jnp.float32),
            pltpu.SemaphoreType.DMA((2, TILES)),
        ]
        + second,
        compiler_params=pltpu.CompilerParams(vmem_limit_bytes=24 << 20),
        cost_estimate=pl.CostEstimate(
            flops=6_000_000_000, bytes_accessed=4_000_000, transcendentals=4_000_000
        ),
        name="attend",
    )(tab, in_hbm(received) if part else received, *state)


def project_kernel(order, mine, theirs, w, base, o, ws, acc, sem):
    copies = []
    for k in range(8):
        rows = pl.ds(pl.multiple_of(order[k] * 512, 512), 512)
        copies.append(pltpu.make_async_copy(w.at[rows], ws.at[k], sem.at[k]))
        copies[-1].start()
    for k in range(8):
        part = (mine if k < 4 else theirs)[k % 4, 0 : acc.shape[0]]
        copies[k].wait()
        term = jnp.dot(part, ws[k], preferred_element_type=jnp.float32)
        if k == 0:
            acc[...] = base[...].astype(jnp.float32) + term
        elif k < 7:
            acc[...] += term
        else:
            total = (acc[...] + term).astype(jnp.bfloat16)
            o[...] = total.reshape(o.shape)


def project(order, mine, theirs, w, base, shape):
    rows = base.shape[0]
    vmem = pl.BlockSpec(memory_space=pltpu.VMEM)
    hbm = pl.BlockSpec(memory_space=pltpu.HBM)
    return pl.pallas_call(
        project_kernel,
        in_specs=[pl.BlockSpec(memory_space=pltpu.SMEM), vmem, vmem, hbm, vmem],
        out_specs=vmem,
        out_shape=jax.ShapeDtypeStruct(shape, jnp.bfloat16),
        scratch_shapes=[
            pltpu.VMEM((8, 512, 1024), jnp.bfloat16),
            pltpu.VMEM((rows, 1024), jnp.float32),
            pltpu.SemaphoreType.DMA((8,)),
        ],
        compiler_params=pltpu.CompilerParams(vmem_limit_bytes=24 << 20),
        cost_estimate=pl.CostEstimate(
            flops=rows * 8_388_608, bytes_accessed=8_388_608 + rows * 12_288, transcendentals=0
        ),
        name="project",
    )(order, mine, theirs, in_hbm(w), base)


def experts_kernel(piece, gate, up, down, o, gs, us, ds, out, sem):
    wide = D // 4
    copies = []
    for k in range(4):
        span = pl.ds(k * wide, wide)
        copies.append(
            (
                pltpu.make_async_copy(gate.at[0, span], gs.at[k], sem.at[0, k]),
                pltpu.make_async_copy(up.at[0, span], us.at[k], sem.at[1, k]),
            )
        )
    last = [
        pltpu.make_async_copy(down.at[0, :, pl.ds(k * wide, wide)], ds.at[k], sem.at[2, k])
        for k in range(4)
    ]
    for group in (*copies, last):
        for copy in group:
            copy.start()
    g = u = None
    for k in range(4):
        for copy in copies[k]:
            copy.wait()
        rows = piece[:, k * wide : (k + 1) * wide]
        add_g = jnp.dot(rows, gs[k], preferred_element_type=jnp.float32)
        add_u = jnp.dot(rows, us[k], preferred_element_type=jnp.float32)
        g, u = (add_g, add_u) if k == 0 else (g + add_g, u + add_u)
    inner = (jax.nn.silu(g) * u).astype(jnp.bfloat16)
    for k in range(4):
        last[k].wait()
        out[k] = jnp.dot(inner, ds[k], preferred_element_type=jnp.float32).astype(o.dtype)
        written = pltpu.make_async_copy(
            out.at[k], o.at[:, pl.ds(k * wide, wide)], sem.at[3, k]
        )
        written.start()
        last[k] = written
    for written in last:
        written.wait()


def experts(piece, w_gate, w_up, w_down):
    hbm = pl.BlockSpec(memory_space=pltpu.HBM)
    return pl.pallas_call(
        experts_kernel,
        in_specs=[pl.BlockSpec(memory_space=pltpu.VMEM)] + [hbm] * 3,
        out_specs=hbm,
        out_shape=pltpu.HBM((128, D), jnp.bfloat16),
        scratch_shapes=[
            pltpu.VMEM((4, D // 4, 256), jnp.bfloat16),
            pltpu.VMEM((4, D // 4, 256), jnp.bfloat16),
            pltpu.VMEM((4, 256, D // 4), jnp.bfloat16),
            pltpu.VMEM((4, 128, D // 4), jnp.bfloat16),
            pltpu.SemaphoreType.DMA((4, 4)),
        ],
        compiler_params=pltpu.CompilerParams(vmem_limit_bytes=24 << 20),
        cost_estimate=pl.CostEstimate(
            flops=1_610_000_000, bytes_accessed=16_800_000, transcendentals=32_768
        ),
        name="experts",
    )(piece, in_hbm(w_gate), in_hbm(w_up), in_hbm(w_down))


def add_kernel(parts, o):
    total = parts[0].astype(jnp.float32)
    for n in range(1, 4):
        total += parts[n].astype(jnp.float32)
    o[...] = total.astype(o.dtype)


def add(parts):
    rows, width = parts.shape[1] // 4, parts.shape[2]
    return pl.pallas_call(
        add_kernel,
        grid=(4,),
        in_specs=[pl.BlockSpec((4, rows, width), lambda k: (0, k, 0))],
        out_specs=pl.BlockSpec((rows, width), lambda k: (k, 0)),
        out_shape=jax.ShapeDtypeStruct(parts.shape[1:], jnp.bfloat16),
        compiler_params=pltpu.CompilerParams(vmem_limit_bytes=8 << 20),
        name="add",
    )(parts)


def swap(array):
    return lax.ppermute(array, "c", [(0, 1), (1, 0)])


def ring(array, step):
    return lax.ppermute(array, "y", [(i, (i + step) % 4) for i in range(4)])


def in_three(array):
    parts = []
    for _ in range(3):
        part = lax.reduce_precision(array, 8, 7)
        parts.append(part.astype(jnp.bfloat16))
        array = array - part
    return parts


def shards(
    residual,
    queries,
    keys,
    values,
    documents,
    out_proj,
    modality,
    norm_gain,
    picks,
    router,
    w_gate,
    w_up,
    w_down,
):
    z, x, y, c = (lax.axis_index(name) for name in ALL)
    seq = z * 4 + x
    expert = y * 2 + c
    b = jnp.where(c == 0, x, z)

    got = exchange(pack_heads(queries, keys, values), GROUP_A)
    one, two = pack_parts(got)
    one = exchange(one, GROUP_B).reshape(8, 1280, HD)
    one, two = lax.optimization_barrier((one, two))
    two = exchange(two, GROUP_B).reshape(8, 1024, HD)

    index = jnp.arange(BLOCKS, dtype=jnp.int32)
    low, high = index % 4, index // 4
    from_a = jnp.where(c == 0, high, low)
    from_b = jnp.where(c == 0, low, high)
    bound = documents.shape[0] - jnp.sum(documents)
    tab = jnp.concatenate(
        [
            from_b * 2 + from_a % 2,
            from_a * 4 + from_b,
            from_a // 2,
            jnp.stack([bound, b, c]).astype(jnp.int32),
        ]
    ).astype(jnp.int32)
    ranked = picks.reshape(8, 8, 16)
    inside = (ranked // TOK) == seq
    local = jnp.sum(jnp.where(inside, ranked - seq * TOK, 0), axis=1).T.reshape(128, 1)
    filled = jnp.any(inside, axis=1).T.reshape(128, 1)
    hot = ((jnp.arange(TOK, dtype=jnp.int32)[None, :] == local) & filled).astype(jnp.bfloat16)

    base = jnp.dot(hot, residual, preferred_element_type=jnp.float32).astype(jnp.bfloat16)
    gain_sent = jnp.stack(in_three(norm_gain), axis=1).reshape(12, 512)
    gain_sent = jnp.pad(gain_sent, ((0, 4), (0, 0)))

    state = attend(0, tab, one)
    attended = attend(1, tab, two, *state)
    attended = exchange(attended, GROUP_AB)
    attended, hot, base, gain_sent = lax.optimization_barrier((attended, hot, base, gain_sent))
    attended = attended.reshape(4, TOK, HD).transpose(1, 0, 2).reshape(TOK, 4 * HD)

    early = jnp.dot(hot, attended, preferred_element_type=jnp.float32).astype(jnp.bfloat16)
    early = jnp.concatenate([early, gain_sent], axis=0)
    mine = lax.all_to_all(jnp.broadcast_to(early[None], (4, 144, 512)), "y", 0, 0, tiled=True)
    theirs = swap(mine)
    chip = jnp.arange(4, dtype=jnp.int32)
    order = jnp.concatenate([2 * chip + c, 2 * chip + 1 - c]).astype(jnp.int32)
    rows = project(order, mine, theirs, out_proj, base, (128, 8, 128))
    gains = jnp.stack([mine[:, 128:140], theirs[:, 128:140]]).reshape(2, 4, 2, 3, 1024)
    gains = jnp.where(expert < 4, gains[:, :, 0], gains[:, :, 1]).astype(jnp.float32)
    gains = gains[:, :, 0] + (gains[:, :, 1] + gains[:, :, 2])
    gains = jnp.where(c == 0, gains, gains[::-1])
    gain = gains.transpose(1, 0, 2).reshape(1, D)

    held, rows = lax.optimization_barrier((attended, rows))
    arrived = lax.all_to_all(rows, ALL, 0, 0, tiled=True)
    before = ring(held, 1)
    after = ring(held, -1)
    half = TOK // 2
    opposite = jnp.concatenate([ring(before[:half], 1), ring(after[half:], -1)], axis=0)
    mine = jnp.stack([held, before, after, opposite])
    theirs = swap(mine)
    chip = jnp.remainder(y + jnp.array([0, 3, 1, 2], jnp.int32), 4)
    order = jnp.concatenate([2 * chip + c, 2 * chip + 1 - c]).astype(jnp.int32)
    own = lax.dynamic_index_in_dim(ranked, expert, 0, keepdims=False)
    own = lax.dynamic_index_in_dim(own, seq, 1, keepdims=False)
    source = (own // TOK)[:, None] == jnp.arange(16, dtype=jnp.int32)[None, :]
    source = source.astype(jnp.bfloat16)
    taken = jnp.dot(source, arrived.reshape(16, D), preferred_element_type=jnp.float32)
    inverse = lax.rsqrt(jnp.mean(taken * taken, axis=1, keepdims=True) + 1e-05)
    chosen = (taken * inverse * gain).astype(jnp.bfloat16)
    logits = jnp.dot(chosen, router, preferred_element_type=jnp.float32)
    near = spread(chosen, GROUP_A)
    far = spread(near.reshape(32, D), GROUP_B)
    piece = far.reshape(128, D)
    partial = experts(piece, w_gate, w_up, w_down)
    partial = exchange(partial.reshape(4, 32, D), GROUP_B)
    partial = add(partial)
    partial = exchange(partial.reshape(4, 8, D), GROUP_A)
    summed = jnp.sum(partial.astype(jnp.float32), axis=0)
    weighted = (jax.nn.sigmoid(logits) * summed).astype(jnp.bfloat16)
    back = lax.dot_general(
        source, weighted, (((0,), (0,)), ((), ())), preferred_element_type=jnp.float32
    ).astype(jnp.bfloat16)
    back, mine, theirs = lax.optimization_barrier((back, mine, theirs))
    hidden = project(order, mine, theirs, out_proj, residual, (TOK, 1024))
    returned = lax.all_to_all(back.reshape(128, 8, 128), ALL, 0, 0, tiled=True)
    expert_add = lax.dot_general(
        hot, returned.reshape(128, 1024), (((0,), (0,)), ((), ())), preferred_element_type=jnp.float32
    )
    return (hidden.astype(jnp.float32) + expert_add).astype(jnp.bfloat16)


def solution(mesh):
    finer = Mesh(mesh.devices.reshape(4, 4, 4, 2), ALL)
    in_specs = (
        P(SEQ, EXP),
        P(SEQ, EXP),
        P(SEQ, EXP),
        P(SEQ, EXP),
        P(),
        P(None, EXP),
        P(SEQ),
        P(None, EXP),
        P(),
        P(None, EXP),
        P(EXP, None, SEQ),
        P(EXP, None, SEQ),
        P(EXP, SEQ, None),
    )
    return jax.shard_map(
        shards, mesh=finer, in_specs=in_specs, out_specs=P(SEQ, EXP), check_vma=False
    )
```
